32 devices in a mesh: groups: 2 (over x), seq: 8 (over z, y), head: 2 (over core).
Axes of the slice: x: 2, y: 2, z: 4, core: 2. Of those that a mesh axis runs over, the one named last changes fastest.
Arguments:
- queries: float32 [4096, 2048], P(('groups', 'seq'), 'head'), parts along dimension 0, may hold values from -6 to 6
- keys: float32 [4096, 2048], P(('groups', 'seq'), 'head'), parts along dimension 0, may hold values from -0.01171875 to 0.01171875
- values: float32 [4096, 2048], P(('groups', 'seq'), 'head'), parts along dimension 0, may hold values from -6 to 6
- level_weight: float32 [16, 6, 4096], P('head', None, ('groups', 'seq')), parts along dimension 2, may hold values from 0.1 to 1
- prefix_weight: float32 [16, 8, 4096], P('head', None, ('groups', 'seq')), parts along dimension 2, may hold values from 0.1 to 1
- prefix_state: float32 [16, 2048, 128], P('head', 'groups'), parts along dimension 1, may hold values from -0.5 to 0.5
Outputs:
- attended: float32 [4096, 2048], P(('groups', 'seq'), 'head'), parts along dimension 0
The draws below stay inside these ranges and needn't reach their ends.
There are 2 independent parts, one for each index of `groups`. The reference program is written for one: setup_inputs(seed, part) draws one part's arguments, and reference() takes and returns one part's arrays. A program takes and returns all parts, laid end to end along the dimension named above; each array names one. Nothing has to cross between parts.
All inputs are finite; a program needn't handle non-finite values.
Results may differ from the reference program's by a relative error of at most 0.00005.
Values sent between devices are 32-bit elements; how exact they have to be, the bound alone decides.
No kernel may reach another device: no remote copies, remote signals or barrier semaphores. Data moves between devices by JAX's collectives and lax.ppermute only.
A program may use at most 128 MiB of HBM per device.

```python
import jax
import jax.numpy as jnp
from jax import lax

H = 16
DH = 128
LEVELS = 6
BUCKETS = 8
TOK_DEV = 256
TOKENS = 2048
N_SEQ = 8


def level_of(rng, extent, pieces, least, high):
    loudness, own = 1.0, jax.random.fold_in(rng, 6)
    for position, parts in pieces:
        heights = jnp.exp(jax.random.uniform(jax.random.fold_in(own, position), (parts,), jnp.float32, least / len(pieces), high / len(pieces)))
        loudness = loudness * jnp.repeat(heights, extent[position] // parts).reshape([-1 if axis == position else 1 for axis in range(len(extent))])
    return loudness


def bell_draw(key, shape, spread, limit, cuts=(), kind=jnp.bfloat16):
    level = level_of(key, shape, cuts, -0.22, 0.18) if cuts else 1.0
    values = jax.random.normal(key, shape, jnp.float32) * spread * level
    return jnp.minimum(jnp.maximum(values, -limit), limit).astype(kind)


def setup_inputs(seed: int = 0, part: int = 0) -> dict:
    streams_of = jax.random.split(jax.random.key(seed), 7)
    part_splits = jax.random.split(jax.random.fold_in(streams_of[6], part), 7)
    return {
        "queries": bell_draw(part_splits[0], (TOKENS, H * DH), 1.0, 6.0, ((0, 8), (1, 2)), jnp.float32),
        "keys": bell_draw(part_splits[1], (TOKENS, H * DH), ((DH * TOKENS) ** -0.5), 0.01171875, ((0, 8), (1, 2)), jnp.float32),
        "values": bell_draw(part_splits[2], (TOKENS, H * DH), 1.0, 6.0, ((0, 8), (1, 2)), jnp.float32),
        "level_weight": jnp.clip(0.1 + 0.9 * jax.random.uniform(part_splits[3], (H, LEVELS, TOKENS), jnp.float32) ** level_of(part_splits[3], (H, LEVELS, TOKENS), ((0, 2), (2, 8)), -0.2, 0.2), 0.1, 1.0),
        "prefix_weight": jnp.clip(0.1 + 0.9 * jax.random.uniform(part_splits[4], (H, BUCKETS, TOKENS), jnp.float32) ** level_of(part_splits[4], (H, BUCKETS, TOKENS), ((0, 2), (2, 8)), -0.2, 0.2), 0.1, 1.0),
        "prefix_state": bell_draw(part_splits[5], (H, BUCKETS * DH, DH), DH ** -0.5, 0.5, ((0, 2),), jnp.float32),
    }


def bucket_select():
    block_ids = jnp.arange(N_SEQ, dtype=jnp.int32)
    differing = jnp.bitwise_xor(block_ids[:, None], block_ids[None, :])
    bucket_level_number = sum((jnp.right_shift(differing, shift_by) > 0).astype(jnp.int32) for shift_by in range(LEVELS))
    level_ids = jnp.arange(1, LEVELS, dtype=jnp.int32)
    earlier = (block_ids[None, :] < block_ids[:, None])[:, None, :]
    return earlier & (bucket_level_number[:, None, :] == level_ids[None, :, None])


def one_head(inputs):
    query_heads, key_head_count, value_heads, level_rows, prefix_rows, prefix_mats = inputs
    highest_level = lax.Precision.HIGHEST
    level_selection_mask = bucket_select().astype(query_heads.dtype)
    block_memory_state = jnp.einsum('ctd,cte->cde', key_head_count, value_heads, precision=highest_level)
    per_level_states = jnp.einsum('qov,vfn->qofn', level_selection_mask, block_memory_state, precision=highest_level)
    query_key_scores = jnp.einsum('ctd,csd->cts', query_heads, key_head_count, precision=highest_level)
    row_index = lax.broadcasted_iota(jnp.int32, (TOK_DEV, TOK_DEV), 0)
    col_index = lax.broadcasted_iota(jnp.int32, (TOK_DEV, TOK_DEV), 1)
    causal = col_index <= row_index
    query_key_scores = jnp.where(causal[None], query_key_scores, jnp.zeros_like(query_key_scores)) * level_rows[0][:, :, None]
    local_out = jnp.einsum('cts,cse->cte', query_key_scores, value_heads, precision=highest_level)
    scaled = query_heads[:, None] * jnp.transpose(level_rows[1:], (1, 0, 2))[..., None]
    level_out = jnp.einsum('cltd,clde->cte', scaled, per_level_states, precision=highest_level)
    weighted = query_heads[None] * prefix_rows[..., None]
    prefix_out = jnp.einsum('bctd,bde->cte', weighted, prefix_mats, precision=highest_level)
    return local_out + level_out + prefix_out


def reference(queries, keys, values, level_weight, prefix_weight, prefix_state):
    def split_heads(array):
        return jnp.transpose(array.reshape(N_SEQ, TOK_DEV, H, DH), (2, 0, 1, 3))

    level_rows = level_weight.reshape(H, LEVELS, N_SEQ, TOK_DEV)
    prefix_rows = prefix_weight.reshape(H, BUCKETS, N_SEQ, TOK_DEV)
    prefix_mats = prefix_state.reshape(H, BUCKETS, DH, DH)
    attention_output = lax.map(one_head, (split_heads(queries), split_heads(keys), split_heads(values), level_rows, prefix_rows, prefix_mats))
    return jnp.transpose(attention_output, (1, 2, 0, 3)).reshape(TOKENS, H * DH)
```

```python
import functools

import jax
import jax.numpy as jnp
from jax import lax
from jax.experimental import pallas as pl
from jax.experimental.pallas import tpu as pltpu
from jax.sharding import PartitionSpec as P

DH = 128
BF16 = jnp.bfloat16
F32 = jnp.float32
VMEM_LIMIT = 40 * 1024 * 1024


def split(x):
    high = x.astype(BF16)
    low = (x - high.astype(F32)).astype(BF16)
    return high, low


def beside(x):
    return jnp.concatenate(split(x), axis=1)


def fold_columns(x):
    half = x.shape[1] // 2
    return x[:, :half] + x[:, half:]


def outer_state(k, v):
    full = lax.dot_general(
        beside(k), beside(v), (((0,), (0,)), ((), ())), preferred_element_type=F32
    )
    full = fold_columns(full)
    return full[:DH] + full[DH:]


def through_state(scaled, state):
    wide = beside(state)
    return jnp.dot(
        beside(scaled), jnp.concatenate([wide, wide], axis=0), preferred_element_type=F32
    )


def states_kernel(flip, chunks, k_hbm, v_hbm, *refs):
    outs = refs[:chunks]
    k_buf, v_buf, sems = refs[chunks:]
    width = k_buf.shape[2]
    odd = lax.rem(lax.axis_index("seq"), 2)
    half = odd if flip else 1 - odd
    copies = []
    for c in range(chunks):
        columns = pl.ds(pl.multiple_of((half * chunks + c) * width, DH), width)
        pair = (
            pltpu.make_async_copy(k_hbm.at[:, columns], k_buf.at[c], sems.at[0, c]),
            pltpu.make_async_copy(v_hbm.at[:, columns], v_buf.at[c], sems.at[1, c]),
        )
        for copy in pair:
            copy.start()
        copies.append(pair)
    for c in range(chunks):
        for copy in copies[c]:
            copy.wait()
        for j in range(width // DH):
            at = slice(j * DH, (j + 1) * DH)
            outs[c][j] = outer_state(k_buf[c, :, at], v_buf[c, :, at])


def block_states(keys, values, flip, chunks):
    rows, columns = keys.shape
    width = columns // (2 * chunks)
    shape = jax.ShapeDtypeStruct((width // DH, DH, DH), F32)
    return pl.pallas_call(
        functools.partial(states_kernel, flip, chunks),
        out_shape=[shape] * chunks,
        in_specs=[pl.BlockSpec(memory_space=pl.ANY)] * 2,
        out_specs=[pl.BlockSpec(memory_space=pltpu.VMEM)] * chunks,
        scratch_shapes=[
            pltpu.VMEM((chunks, rows, width), F32),
            pltpu.VMEM((chunks, rows, width), F32),
            pltpu.SemaphoreType.DMA((2, chunks)),
        ],
        compiler_params=pltpu.CompilerParams(vmem_limit_bytes=VMEM_LIMIT),
        cost_estimate=pl.CostEstimate(
            flops=8 * rows * width * chunks * DH,
            bytes_accessed=8 * rows * width * chunks,
            transcendentals=0,
        ),
        name="states_flip" if flip else "states_own",
    )(keys, values)


def base_kernel(q_ref, k_ref, v_ref, level_ref, bucket_ref, prefix_ref, out_ref):
    q, k, v = q_ref[...], k_ref[...], v_ref[...]
    rows = q.shape[0]
    buckets = bucket_ref.shape[1]
    k_high, k_low = split(k)
    q_wide = beside(q)
    nt = (((1,), (1,)), ((), ()))
    scores = lax.dot_general(
        q_wide, jnp.concatenate([k_high, k_high], axis=1), nt, preferred_element_type=F32
    ) + lax.dot_general(
        q_wide, jnp.concatenate([k_low, k_low], axis=1), nt, preferred_element_type=F32
    )
    row = lax.broadcasted_iota(jnp.int32, (rows, rows), 0)
    column = lax.broadcasted_iota(jnp.int32, (rows, rows), 1)
    level = jnp.transpose(level_ref[0])
    bucket = jnp.transpose(bucket_ref[0])
    scores = jnp.where(column <= row, scores, 0.0) * level[:, 0:1]
    scores_high, scores_low = split(scores)
    v_wide = beside(v)
    total = jnp.dot(scores_high, v_wide, preferred_element_type=F32)
    total += jnp.dot(scores_low, v_wide, preferred_element_type=F32)
    for b in range(buckets):
        total += through_state(
            q * bucket[:, b : b + 1], prefix_ref[0, b * DH : (b + 1) * DH, :]
        )
    out_ref[...] = fold_columns(total)


def base_part(queries, keys, values, level_weight, prefix_weight, prefix_state):
    rows, columns = queries.shape
    heads = columns // DH
    by_head = lambda shape: pl.BlockSpec((1, *shape[1:]), lambda h: (h, 0, 0))
    column_block = pl.BlockSpec((rows, DH), lambda h: (0, h))
    return pl.pallas_call(
        base_kernel,
        out_shape=jax.ShapeDtypeStruct((rows, columns), F32),
        grid=(heads,),
        in_specs=[
            column_block,
            column_block,
            column_block,
            by_head(level_weight.shape),
            by_head(prefix_weight.shape),
            by_head(prefix_state.shape),
        ],
        out_specs=column_block,
        compiler_params=pltpu.CompilerParams(
            dimension_semantics=("arbitrary",), vmem_limit_bytes=VMEM_LIMIT
        ),
        cost_estimate=pl.CostEstimate(
            flops=2 * heads * rows * rows * 256 * 12,
            bytes_accessed=16 * rows * columns + 4 * prefix_state.size,
            transcendentals=0,
        ),
        name="base_part",
    )(queries, keys, values, level_weight, prefix_weight, prefix_state)


def levels_kernel(first, count, side_ref, q_ref, level_ref, *refs):
    state_refs = refs[:count]
    in_ref, out_ref = refs[count:]
    q = q_ref[...]
    level = jnp.transpose(level_ref[0])
    total = None
    for i in range(count):
        take = side_ref[1 + first + i].astype(F32)
        weight = level[:, 1 + first + i : 2 + first + i] * take
        term = through_state(q * weight, state_refs[i][0])
        total = term if total is None else total + term
    out_ref[...] = in_ref[...] + fold_columns(total)


def add_levels(side, queries, level_weight, total, states, first, place, name):
    rows, _ = queries.shape
    heads = states[0].shape[0]
    column_block = pl.BlockSpec((rows, DH), lambda h, s: (0, place(h, s)))
    return pl.pallas_call(
        functools.partial(levels_kernel, first, len(states)),
        out_shape=jax.ShapeDtypeStruct(total.shape, F32),
        grid_spec=pltpu.PrefetchScalarGridSpec(
            num_scalar_prefetch=1,
            grid=(heads,),
            in_specs=[
                column_block,
                pl.BlockSpec((1, *level_weight.shape[1:]), lambda h, s: (place(h, s), 0, 0)),
                *[pl.BlockSpec((1, DH, DH), lambda h, s: (h, 0, 0))] * len(states),
                column_block,
            ],
            out_specs=column_block,
        ),
        input_output_aliases={3 + len(states): 0},
        compiler_params=pltpu.CompilerParams(
            dimension_semantics=("arbitrary",), vmem_limit_bytes=VMEM_LIMIT
        ),
        cost_estimate=pl.CostEstimate(
            flops=2 * heads * rows * 256 * 256 * len(states),
            bytes_accessed=4 * heads * (3 * rows * DH + len(states) * DH * DH),
            transcendentals=0,
        ),
        name=name,
    )(side, queries, level_weight, *states, total)


def swapped(array, bit):
    size = lax.axis_size("seq")
    return lax.ppermute(array, "seq", [(i, i ^ 1 << bit) for i in range(size)])


def shards(queries, keys, values, level_weight, prefix_weight, prefix_state):
    heads = queries.shape[1] // DH
    levels = lax.axis_size("seq").bit_length() - 1
    chunks = 2
    per = heads // (2 * chunks)
    position = lax.axis_index("seq").astype(jnp.int32)
    side = jnp.stack([position & 1] + [(position >> b) & 1 for b in range(levels)])

    given = block_states(keys, values, True, chunks)
    received = [swapped(x, 0) for x in given]
    own = block_states(keys, values, False, chunks)
    total = base_part(queries, keys, values, level_weight, prefix_weight, prefix_state)

    own_states = [received]
    running = [a + b for a, b in zip(own, received)]
    for bit in range(1, levels):
        arrived = [swapped(x, bit) for x in running]
        own_states.append(arrived)
        running = [a + b for a, b in zip(running, arrived)]
    other_states = [[swapped(x, 0) for x in own]]
    for arrived in own_states[1:]:
        other_states.append([swapped(x, 0) for x in arrived])

    def own_place(c):
        return lambda h, s: (1 - s[0]) * (chunks * per) + c * per + h

    def other_place(c):
        return lambda h, s: s[0] * (chunks * per) + c * per + h

    for c in range(chunks):
        total = add_levels(
            side, queries, level_weight, total, [x[c] for x in own_states], 0, own_place(c), f"own{c}"
        )
    if levels > 1:
        for c in range(chunks):
            total = add_levels(
                side, queries, level_weight, total, [x[c] for x in other_states[:-1]], 0, other_place(c), f"other{c}"
            )
    for c in range(chunks):
        total = add_levels(
            side,
            queries,
            level_weight,
            total,
            [other_states[-1][c]],
            levels - 1,
            other_place(c),
            f"last{c}",
        )
    return total


def solution(mesh):
    return jax.shard_map(
        shards,
        mesh=mesh,
        in_specs=(
            P(("groups", "seq"), "head"),
            P(("groups", "seq"), "head"),
            P(("groups", "seq"), "head"),
            P("head", None, ("groups", "seq")),
            P("head", None, ("groups", "seq")),
            P("head", "groups", None),
        ),
        out_specs=P(("groups", "seq"), "head"),
        check_vma=False,
    )
```

```python
import functools

import jax
import jax.numpy as jnp
from jax import lax
from jax.experimental import pallas as pl
from jax.experimental.pallas import tpu as pltpu
from jax.sharding import PartitionSpec as P

DH = 128
BF16 = jnp.bfloat16
F32 = jnp.float32
PARTS = 2
GRANT = 67043328
IN_VMEM = pl.BlockSpec(memory_space=pltpu.VMEM)
IN_HBM = pl.BlockSpec(memory_space=pltpu.HBM)


def split(x):
    high = x.astype(BF16)
    low = (x - high.astype(F32)).astype(BF16)
    return high, low


def beside(x):
    return jnp.concatenate(split(x), axis=1)


def fold_columns(x):
    half = x.shape[1] // 2
    return x[:, :half] + x[:, half:]


def outer_state(k, v):
    full = lax.dot_general(
        beside(k), beside(v), (((0,), (0,)), ((), ())), preferred_element_type=F32
    )
    full = fold_columns(full)
    return full[:DH] + full[DH:]


def through_state(scaled, state):
    wide = beside(state)
    return jnp.dot(
        beside(scaled), jnp.concatenate([wide, wide], axis=0), preferred_element_type=F32
    )


def first_head(place, per):
    own = 1 - lax.rem(lax.axis_index("seq"), 2)
    half = own if place < PARTS else 1 - own
    return (half * PARTS + place % PARTS) * per


def head_columns(head, count=1):
    return pl.ds(pl.multiple_of(head * DH, DH), count * DH)


def given_kernel(k_hbm, v_hbm, *refs):
    outs = refs[:PARTS]
    k_buf, v_buf, sems = refs[PARTS:]
    per = outs[0].shape[0]
    copies = []
    for c in range(PARTS):
        columns = head_columns(first_head(PARTS + c, per), per)
        pair = (
            pltpu.make_async_copy(k_hbm.at[:, columns], k_buf.at[c], sems.at[0, c]),
            pltpu.make_async_copy(v_hbm.at[:, columns], v_buf.at[c], sems.at[1, c]),
        )
        for copy in pair:
            copy.start()
        copies.append(pair)
    for c in range(PARTS):
        for copy in copies[c]:
            copy.wait()
        for j in range(per):
            at = slice(j * DH, (j + 1) * DH)
            outs[c][j] = outer_state(k_buf[c, :, at], v_buf[c, :, at])


def given_states(keys, values):
    rows, columns = keys.shape
    width = columns // (2 * PARTS)
    return pl.pallas_call(
        given_kernel,
        out_shape=[jax.ShapeDtypeStruct((width // DH, DH, DH), F32)] * PARTS,
        in_specs=[IN_HBM] * 2,
        out_specs=[IN_VMEM] * PARTS,
        scratch_shapes=[
            pltpu.VMEM((PARTS, rows, width), F32),
            pltpu.VMEM((PARTS, rows, width), F32),
            pltpu.SemaphoreType.DMA((2, PARTS)),
        ],
        compiler_params=pltpu.CompilerParams(vmem_limit_bytes=GRANT - columns * DH * 5),
        cost_estimate=pl.CostEstimate(
            flops=4 * rows * columns * DH, bytes_accessed=4 * rows * columns, transcendentals=0
        ),
        name="states_given",
    )(keys, values)


def own_kernel(
    level_ref, bucket_ref, q_hbm, k_hbm, v_hbm, q_out, k_out, v_out, weight_ref, whole_ref, *refs
):
    part_refs, sems = refs[:-1], refs[-1]
    per = part_refs[0].shape[0]
    half = PARTS * per
    copies = []
    for i, (source, to) in enumerate(((k_hbm, k_out), (v_hbm, v_out), (q_hbm, q_out))):
        for h in range(2):
            copy = pltpu.make_async_copy(
                source.at[:, head_columns(first_head(h * PARTS, per), half)],
                to.at[:, h * half * DH : (h + 1) * half * DH],
                sems.at[i, h],
            )
            copy.start()
            copies.append(copy)
    position = lax.axis_index("seq")
    own_second = lax.rem(position, 2) == 0
    levels, heads, rows = level_ref.shape
    buckets = bucket_ref.shape[1]
    lines = []
    for i in range(levels):
        line = level_ref[i]
        if i:
            line = line * lax.rem(lax.shift_right_logical(position, i - 1), 2).astype(F32)
        lines.append(jnp.where(own_second, jnp.concatenate([line[half:], line[:half]], axis=0), line))
    first = jnp.where(own_second, half, 0)
    for h in range(heads):
        lines.append(bucket_ref[lax.rem(first + h, heads)])
    spare = weight_ref.shape[1] - heads * (levels + buckets)
    if spare:
        lines.append(jnp.zeros((spare, rows), F32))
    weight_ref[...] = jnp.transpose(jnp.concatenate(lines, axis=0))

    copies[0].wait()
    copies[2].wait()
    for c, part_ref in enumerate(part_refs):
        for j in range(per):
            at = slice((c * per + j) * DH, (c * per + j + 1) * DH)
            state = outer_state(k_out[:, at], v_out[:, at])
            part_ref[j] = state
            whole_ref[c * per + j] = state
    for i in (1, 3, 4, 5):
        copies[i].wait()


def own_block_states(queries, keys, values, level_weight, prefix_weight):
    rows, columns = keys.shape
    heads = columns // DH
    per = heads // (2 * PARTS)
    weights = heads * (level_weight.shape[1] + prefix_weight.shape[1])
    shapes = [queries.shape, keys.shape, values.shape, (rows, pl.cdiv(weights, DH) * DH)]
    shapes += [(PARTS * per, DH, DH)] + [(per, DH, DH)] * PARTS
    return pl.pallas_call(
        own_kernel,
        out_shape=[jax.ShapeDtypeStruct(s, F32) for s in shapes],
        in_specs=[IN_VMEM] * 2 + [IN_HBM] * 3,
        out_specs=[IN_VMEM] * len(shapes),
        scratch_shapes=[pltpu.SemaphoreType.DMA((3, 2))],
        compiler_params=pltpu.CompilerParams(vmem_limit_bytes=GRANT - 14 * rows * columns * 4),
        cost_estimate=pl.CostEstimate(
            flops=4 * rows * columns * DH, bytes_accessed=24 * rows * columns, transcendentals=0
        ),
        name="states_own",
    )(jnp.transpose(level_weight, (1, 0, 2)), prefix_weight, queries, keys, values)


def base_kernel(place, levels, buckets, q_ref, k_ref, v_ref, weight_ref, prefix_hbm, out_ref, buf, sems):
    rows = q_ref.shape[0]
    heads = prefix_hbm.shape[0]
    per = out_ref.shape[1] // DH
    start = first_head(place, per)
    copies = []
    for j in range(per):
        copies.append(pltpu.make_async_copy(prefix_hbm.at[start + j], buf.at[j], sems.at[j]))
        copies[j].start()
    row = lax.broadcasted_iota(jnp.int32, (rows, rows), 0)
    column = lax.broadcasted_iota(jnp.int32, (rows, rows), 1)
    nt = (((1,), (1,)), ((), ()))
    for j in range(per):
        head = place * per + j
        q, k, v = (ref[:, head * DH : (head + 1) * DH] for ref in (q_ref, k_ref, v_ref))
        k_high, k_low = split(k)
        q_wide = beside(q)
        scores = lax.dot_general(
            q_wide, jnp.concatenate([k_high, k_high], axis=1), nt, preferred_element_type=F32
        ) + lax.dot_general(
            q_wide, jnp.concatenate([k_low, k_low], axis=1), nt, preferred_element_type=F32
        )
        scores = jnp.where(column <= row, scores, 0.0) * weight_ref[:, head : head + 1]
        scores_high, scores_low = split(scores)
        v_wide = beside(v)
        total = jnp.dot(scores_high, v_wide, preferred_element_type=F32)
        total += jnp.dot(scores_low, v_wide, preferred_element_type=F32)
        copies[j].wait()
        for b in range(buckets):
            at = heads * levels + head * buckets + b
            total += through_state(
                q * weight_ref[:, at : at + 1], buf[j, b * DH : (b + 1) * DH, :]
            )
        out_ref[:, j * DH : (j + 1) * DH] = fold_columns(total)


def base_part(place, levels, buckets, loaded, prefix_state):
    rows, columns = loaded[0].shape
    width = columns // (2 * PARTS)
    per = width // DH
    return pl.pallas_call(
        functools.partial(base_kernel, place, levels, buckets),
        out_shape=jax.ShapeDtypeStruct((rows, width), F32),
        in_specs=[IN_VMEM] * len(loaded) + [IN_HBM],
        out_specs=IN_VMEM,
        scratch_shapes=[
            pltpu.VMEM((per, *prefix_state.shape[1:]), F32),
            pltpu.SemaphoreType.DMA((per,)),
        ],
        compiler_params=pltpu.CompilerParams(vmem_limit_bytes=GRANT - 16 * rows * columns * 4),
        cost_estimate=pl.CostEstimate(
            flops=2 * width * rows * rows * 24,
            bytes_accessed=16 * rows * width,
            transcendentals=0,
        ),
    )(*loaded, prefix_state)


def levels_kernel(places, first, spread, store, q_ref, weight_ref, *refs):
    count = 1 + max(ref for rows in spread for ref, _ in rows)
    state_refs, refs = refs[:count], refs[count:]
    base_refs, refs = refs[: len(places)], refs[len(places) :]
    per = base_refs[0].shape[1] // DH
    heads = q_ref.shape[1] // DH
    if store:
        out_hbm, buf, sems = refs[-3:]
    copies = []
    for c, place in enumerate(places):
        for j in range(per):
            at = slice(j * DH, (j + 1) * DH)
            head = place * per + j
            q = q_ref[:, head * DH : (head + 1) * DH]
            total = None
            for i, rows in enumerate(spread):
                column = (1 + first + i) * heads + head
                ref, entry = rows[c]
                term = through_state(q * weight_ref[:, column : column + 1], state_refs[ref][entry + j])
                total = term if total is None else total + term
            done = base_refs[c][:, at] + fold_columns(total)
            if store:
                buf[c, :, at] = done
            else:
                refs[c][:, at] = done
        if store:
            columns = head_columns(first_head(place, per), per)
            copy = pltpu.make_async_copy(buf.at[c], out_hbm.at[:, columns], sems.at[c])
            copy.start()
            copies.append(copy)
    for copy in copies:
        copy.wait()


def add_levels(queries, weights, bases, states, spread, places, first, store, out):
    rows, columns = queries.shape
    width = columns // (2 * PARTS)
    count = len(places)
    operands = [queries, weights, *states, *bases]
    in_specs = [IN_VMEM] * len(operands)
    aliases = {}
    if out is not None:
        aliases = {len(operands): 0}
        operands.append(out)
        in_specs.append(IN_HBM)
    shape = (rows, columns) if store else (rows, width)
    return pl.pallas_call(
        functools.partial(levels_kernel, places, first, spread, store),
        out_shape=[jax.ShapeDtypeStruct(shape, F32)] * (1 if store else count),
        in_specs=in_specs,
        out_specs=[IN_HBM if store else IN_VMEM] * (1 if store else count),
        scratch_shapes=[pltpu.VMEM((count, rows, width), F32), pltpu.SemaphoreType.DMA((count,))]
        if store
        else [],
        input_output_aliases=aliases,
        compiler_params=pltpu.CompilerParams(vmem_limit_bytes=GRANT // 4),
        cost_estimate=pl.CostEstimate(
            flops=4 * count * width * rows * rows * len(spread),
            bytes_accessed=12 * rows * width * count,
            transcendentals=0,
        ),
    )(*operands)


def swapped(array, bit, keep=lambda i: True):
    size = lax.axis_size("seq")
    pairs = [(i, i ^ 1 << bit) for i in range(size) if keep(i)]
    return lax.ppermute(array, "seq", pairs)


def attend(queries, keys, values, level_weight, prefix_weight, prefix_state):
    levels = lax.axis_size("seq").bit_length() - 1
    per = queries.shape[1] // DH // (2 * PARTS)
    places = range(PARTS)

    given = given_states(keys, values)
    received = [swapped(given[c], 0) for c in places]
    *loaded, own, part0, part1 = own_block_states(
        queries, keys, values, level_weight, prefix_weight
    )
    parts = (part0, part1)
    query_places, weights = loaded[0], loaded[-1]
    base = []
    for place in range(2 * PARTS):
        base.append(
            base_part(place, level_weight.shape[1], prefix_weight.shape[1], loaded, prefix_state)
        )

    own_states = [list(received)]
    running = [parts[c] + received[c] for c in places]
    for bit in range(1, levels):
        arrived = [swapped(running[c], bit) for c in places]
        own_states.append(arrived)
        running = [a + b for a, b in zip(running, arrived)]
    other_states = [[swapped(own, 0)]]
    for bit in range(1, levels - 1):
        both = jnp.concatenate(own_states[bit], axis=0)
        other_states.append([swapped(both, 0, lambda i: i >> bit & 1)])
    top = levels - 1
    last = [swapped(own_states[top][c], 0, lambda i: i >> top & 1) for c in places]

    spread = [[(i, c * per) for c in places] for i in range(levels - 1)]
    middle = add_levels(
        query_places, weights, base[PARTS:], [x[0] for x in other_states], spread, (2, 3), 0, False, None
    )
    flat = [x for level in own_states for x in level]
    spread = [[(i * PARTS + c, 0) for c in places] for i in range(levels)]
    (out,) = add_levels(query_places, weights, base[:PARTS], flat, spread, (0, 1), 0, True, None)
    for c in places:
        (out,) = add_levels(query_places, weights, [middle[c]], [last[c]], [[(0, 0)]], (PARTS + c,), top, True, out)
    return out


def solution(mesh):
    return jax.shard_map(
        attend,
        mesh=mesh,
        in_specs=(
            P(("groups", "seq"), "head"),
            P(("groups", "seq"), "head"),
            P(("groups", "seq"), "head"),
            P("head", None, ("groups", "seq")),
            P("head", None, ("groups", "seq")),
            P("head", "groups", None),
        ),
        out_specs=P(("groups", "seq"), "head"),
        check_vma=False,
    )
```

```python
import functools

import jax
import jax.numpy as jnp
from jax import lax
from jax.experimental import pallas as pl
from jax.experimental.pallas import tpu as pltpu
from jax.sharding import PartitionSpec as P

DH = 128
BF16 = jnp.bfloat16
F32 = jnp.float32
PARTS = 2
GRANT = 67043328
IN_VMEM = pl.BlockSpec(memory_space=pltpu.VMEM)
IN_HBM = pl.BlockSpec(memory_space=pltpu.HBM)


def split(x):
    high = x.astype(BF16)
    low = (x - high.astype(F32)).astype(BF16)
    return high, low


def beside(x):
    return jnp.concatenate(split(x), axis=1)


def fold_columns(x):
    half = x.shape[1] // 2
    return x[:, :half] + x[:, half:]


def outer_state(k, v):
    full = lax.dot_general(
        beside(k), beside(v), (((0,), (0,)), ((), ())), preferred_element_type=F32
    )
    full = fold_columns(full)
    return full[:DH] + full[DH:]


def through_state(scaled, state):
    wide = beside(state)
    return jnp.dot(
        beside(scaled), jnp.concatenate([wide, wide], axis=0), preferred_element_type=F32
    )


def first_head(place, per):
    own = 1 - lax.rem(lax.axis_index("seq"), 2)
    half = own if place < PARTS else 1 - own
    return (half * PARTS + place % PARTS) * per


def head_columns(head, count=1):
    return pl.ds(pl.multiple_of(head * DH, DH), count * DH)


def given_kernel(k_hbm, v_hbm, *refs):
    outs = refs[:PARTS]
    k_buf, v_buf, sems = refs[PARTS:]
    per = outs[0].shape[0]
    copies = []
    for c in range(PARTS):
        columns = head_columns(first_head(PARTS + c, per), per)
        pair = (
            pltpu.make_async_copy(k_hbm.at[:, columns], k_buf.at[c], sems.at[0, c]),
            pltpu.make_async_copy(v_hbm.at[:, columns], v_buf.at[c], sems.at[1, c]),
        )
        for copy in pair:
            copy.start()
        copies.append(pair)
    for c in range(PARTS):
        for copy in copies[c]:
            copy.wait()
        for j in range(per):
            at = slice(j * DH, (j + 1) * DH)
            outs[c][j] = outer_state(k_buf[c, :, at], v_buf[c, :, at])


def given_states(keys, values):
    rows, columns = keys.shape
    width = columns // (2 * PARTS)
    return pl.pallas_call(
        given_kernel,
        out_shape=[jax.ShapeDtypeStruct((width // DH, DH, DH), F32)] * PARTS,
        in_specs=[IN_HBM] * 2,
        out_specs=[IN_VMEM] * PARTS,
        scratch_shapes=[
            pltpu.VMEM((PARTS, rows, width), F32),
            pltpu.VMEM((PARTS, rows, width), F32),
            pltpu.SemaphoreType.DMA((2, PARTS)),
        ],
        compiler_params=pltpu.CompilerParams(vmem_limit_bytes=GRANT - 107 * rows * columns * 4 // 10),
        cost_estimate=pl.CostEstimate(
            flops=4 * rows * columns * DH, bytes_accessed=4 * rows * columns, transcendentals=0
        ),
        name="states_given",
    )(keys, values)


def own_kernel(
    levels, buckets, line_ref, q_hbm, k_hbm, v_hbm, prefix_hbm,
    q_out, k_out, v_out, prefix_out, weight_ref, whole_ref, *refs,
):
    part_refs, sems = refs[:-1], refs[-1]
    per = part_refs[0].shape[0]
    half = PARTS * per
    copies = []
    for i, (source, to) in enumerate(((k_hbm, k_out), (v_hbm, v_out), (q_hbm, q_out))):
        for h in range(2):
            copy = pltpu.make_async_copy(
                source.at[:, head_columns(first_head(h * PARTS, per), half)],
                to.at[:, h * half * DH : (h + 1) * half * DH],
                sems.at[i, h],
            )
            copy.start()
            copies.append(copy)
    copies.append(pltpu.make_async_copy(prefix_hbm.at[first_head(0, per)], prefix_out, sems.at[3, 0]))
    copies[-1].start()
    position = lax.axis_index("seq")
    own_second = lax.rem(position, 2) == 0
    rows = line_ref.shape[1]
    heads = q_hbm.shape[1] // DH
    lines = []
    for i in range(levels):
        line = line_ref[i * heads : (i + 1) * heads]
        if i:
            line = line * lax.rem(lax.shift_right_logical(position, i - 1), 2).astype(F32)
        lines.append(jnp.where(own_second, jnp.concatenate([line[half:], line[:half]], axis=0), line))
    first = line_ref[heads * levels : heads * levels + half * buckets]
    second = line_ref[heads * levels + half * buckets :]
    lines.append(jnp.where(own_second, second, first))
    lines.append(jnp.where(own_second, first, second))
    spare = weight_ref.shape[1] - heads * (levels + buckets)
    if spare:
        lines.append(jnp.zeros((spare, rows), F32))
    weight_ref[...] = jnp.transpose(jnp.concatenate(lines, axis=0))

    copies[0].wait()
    copies[2].wait()
    for c, part_ref in enumerate(part_refs):
        for j in range(per):
            at = slice((c * per + j) * DH, (c * per + j + 1) * DH)
            state = outer_state(k_out[:, at], v_out[:, at])
            part_ref[j] = state
            whole_ref[c * per + j] = state
    for i in (1, 3, 4, 5, 6):
        copies[i].wait()


def own_block_states(queries, keys, values, level_weight, prefix_weight, prefix_state):
    rows, columns = keys.shape
    heads = columns // DH
    per = heads // (2 * PARTS)
    weights = heads * (level_weight.shape[1] + prefix_weight.shape[1])
    lines = jnp.concatenate(
        [
            jnp.transpose(level_weight, (1, 0, 2)).reshape(-1, rows),
            prefix_weight.reshape(-1, rows),
        ],
        axis=0,
    )
    shapes = [queries.shape, keys.shape, values.shape, prefix_state.shape[1:]]
    shapes += [(rows, pl.cdiv(weights, DH) * DH)]
    shapes += [(PARTS * per, DH, DH)] + [(per, DH, DH)] * PARTS
    return pl.pallas_call(
        functools.partial(own_kernel, level_weight.shape[1], prefix_weight.shape[1]),
        out_shape=[jax.ShapeDtypeStruct(s, F32) for s in shapes],
        in_specs=[IN_VMEM] + [IN_HBM] * 4,
        out_specs=[IN_VMEM] * len(shapes),
        scratch_shapes=[pltpu.SemaphoreType.DMA((4, 2))],
        compiler_params=pltpu.CompilerParams(vmem_limit_bytes=GRANT - 146 * rows * columns * 4 // 10),
        cost_estimate=pl.CostEstimate(
            flops=4 * rows * columns * DH, bytes_accessed=24 * rows * columns, transcendentals=0
        ),
        name="states_own",
    )(lines, queries, keys, values, prefix_state)


def base_kernel(head, per, levels, buckets, q_ref, k_ref, v_ref, weight_ref, prefix_ref, *refs):
    rows = q_ref.shape[0]
    heads = q_ref.shape[1] // DH
    copy = None
    if len(refs) > 1:
        prefix_hbm, out_ref, next_ref, sem = refs
        after = head + 1
        place = first_head(after // per, per) + after % per
        copy = pltpu.make_async_copy(prefix_hbm.at[place], next_ref, sem)
        copy.start()
    else:
        (out_ref,) = refs
    at = slice(head * DH, (head + 1) * DH)
    q, k, v = q_ref[:, at], k_ref[:, at], v_ref[:, at]
    row = lax.broadcasted_iota(jnp.int32, (rows, rows), 0)
    column = lax.broadcasted_iota(jnp.int32, (rows, rows), 1)
    nt = (((1,), (1,)), ((), ()))
    k_high, k_low = split(k)
    q_wide = beside(q)
    scores = lax.dot_general(
        q_wide, jnp.concatenate([k_high, k_high], axis=1), nt, preferred_element_type=F32
    ) + lax.dot_general(
        q_wide, jnp.concatenate([k_low, k_low], axis=1), nt, preferred_element_type=F32
    )
    scores = jnp.where(column <= row, scores, 0.0) * weight_ref[:, head : head + 1]
    scores_high, scores_low = split(scores)
    v_wide = beside(v)
    total = jnp.dot(scores_high, v_wide, preferred_element_type=F32)
    total += jnp.dot(scores_low, v_wide, preferred_element_type=F32)
    for b in range(buckets):
        line = heads * levels + head * buckets + b
        total += through_state(
            q * weight_ref[:, line : line + 1], prefix_ref[b * DH : (b + 1) * DH, :]
        )
    out_ref[...] = fold_columns(total)
    if copy is not None:
        copy.wait()


def base_part(head, per, levels, buckets, loaded, prefix, prefix_state):
    rows, columns = loaded[0].shape
    more = head + 1 < columns // DH
    shapes = [(rows, DH)] + [prefix.shape] * more
    return pl.pallas_call(
        functools.partial(base_kernel, head, per, levels, buckets),
        out_shape=[jax.ShapeDtypeStruct(s, F32) for s in shapes],
        in_specs=[IN_VMEM] * (len(loaded) + 1) + [IN_HBM] * more,
        out_specs=[IN_VMEM] * len(shapes),
        scratch_shapes=[pltpu.SemaphoreType.DMA] * more,
        compiler_params=pltpu.CompilerParams(vmem_limit_bytes=GRANT - 16 * rows * columns * 4),
        cost_estimate=pl.CostEstimate(
            flops=2 * DH * rows * rows * 24,
            bytes_accessed=20 * rows * DH,
            transcendentals=0,
        ),
    )(*loaded, prefix, *[prefix_state] * more)


def levels_kernel(places, first, spread, store, bases, q_ref, weight_ref, *refs):
    count = 1 + max(ref for rows in spread for ref, _ in rows)
    state_refs, refs = refs[:count], refs[count:]
    per = sum(ref.shape[1] for ref in refs[:bases]) // DH // len(places)
    base_refs, refs = refs[:bases], refs[bases:]
    heads = q_ref.shape[1] // DH
    if store:
        out_hbm, buf, sems = refs[-3:]
    copies = []
    for c, place in enumerate(places):
        for j in range(per):
            at = slice(j * DH, (j + 1) * DH)
            head = place * per + j
            q = q_ref[:, head * DH : (head + 1) * DH]
            total = None
            for i, rows in enumerate(spread):
                column = (1 + first + i) * heads + head
                ref, entry = rows[c]
                term = through_state(q * weight_ref[:, column : column + 1], state_refs[ref][entry + j])
                total = term if total is None else total + term
            if bases == len(places):
                before = base_refs[c][:, at]
            else:
                before = base_refs[c * per + j][...]
            done = before + fold_columns(total)
            if store:
                buf[c, :, at] = done
            else:
                refs[c][:, at] = done
        if store:
            columns = head_columns(first_head(place, per), per)
            copy = pltpu.make_async_copy(buf.at[c], out_hbm.at[:, columns], sems.at[c])
            copy.start()
            copies.append(copy)
    for copy in copies:
        copy.wait()


def add_levels(queries, weights, bases, states, spread, places, first, store, out):
    rows, columns = queries.shape
    width = columns // (2 * PARTS)
    count = len(places)
    operands = [queries, weights, *states, *bases]
    in_specs = [IN_VMEM] * len(operands)
    aliases = {}
    if out is not None:
        aliases = {len(operands): 0}
        operands.append(out)
        in_specs.append(IN_HBM)
    shape = (rows, columns) if store else (rows, width)
    return pl.pallas_call(
        functools.partial(levels_kernel, places, first, spread, store, len(bases)),
        out_shape=[jax.ShapeDtypeStruct(shape, F32)] * (1 if store else count),
        in_specs=in_specs,
        out_specs=[IN_HBM if store else IN_VMEM] * (1 if store else count),
        scratch_shapes=[pltpu.VMEM((count, rows, width), F32), pltpu.SemaphoreType.DMA((count,))]
        if store
        else [],
        input_output_aliases=aliases,
        compiler_params=pltpu.CompilerParams(vmem_limit_bytes=GRANT // 4),
        cost_estimate=pl.CostEstimate(
            flops=4 * count * width * rows * rows * len(spread),
            bytes_accessed=12 * rows * width * count,
            transcendentals=0,
        ),
    )(*operands)


def swapped(array, bit, keep=lambda i: True):
    size = lax.axis_size("seq")
    pairs = [(i, i ^ 1 << bit) for i in range(size) if keep(i)]
    return lax.ppermute(array, "seq", pairs)


def attend(queries, keys, values, level_weight, prefix_weight, prefix_state):
    levels = lax.axis_size("seq").bit_length() - 1
    per = queries.shape[1] // DH // (2 * PARTS)
    places = range(PARTS)

    given = given_states(keys, values)
    received = [swapped(given[c], 0) for c in places]
    *loaded, prefix, weights, own, part0, part1 = own_block_states(
        queries, keys, values, level_weight, prefix_weight, prefix_state
    )
    parts = (part0, part1)
    loaded.append(weights)
    query_places = loaded[0]
    base = []
    for head in range(2 * PARTS * per):
        done, *following = base_part(
            head, per, level_weight.shape[1], prefix_weight.shape[1], loaded, prefix, prefix_state
        )
        base.append(done)
        if following:
            (prefix,) = following

    own_states = [list(received)]
    running = [parts[c] + received[c] for c in places]
    for bit in range(1, levels):
        arrived = [swapped(running[c], bit) for c in places]
        own_states.append(arrived)
        running = [a + b for a, b in zip(running, arrived)]
    other_states = [[swapped(own, 0)]]
    for bit in range(1, levels - 1):
        both = jnp.concatenate(own_states[bit], axis=0)
        other_states.append([swapped(both, 0)])
    top = levels - 1
    needs = lambda i: i >> top & 1
    last = [swapped(own_states[top][c], 0, needs if c == PARTS - 1 else lambda i: True) for c in places]

    spread = [[(i, c * per) for c in places] for i in range(levels - 1)]
    middle = add_levels(
        query_places, weights, base[PARTS * per :], [x[0] for x in other_states], spread, (2, 3), 0, False, None
    )
    flat = [x for level in own_states for x in level]
    spread = [[(i * PARTS + c, 0) for c in places] for i in range(levels)]
    (out,) = add_levels(query_places, weights, base[: PARTS * per], flat, spread, (0, 1), 0, True, None)
    for c in places:
        (out,) = add_levels(query_places, weights, [middle[c]], [last[c]], [[(0, 0)]], (PARTS + c,), top, True, out)
    return out


def solution(mesh):
    return jax.shard_map(
        attend,
        mesh=mesh,
        in_specs=(
            P(("groups", "seq"), "head"),
            P(("groups", "seq"), "head"),
            P(("groups", "seq"), "head"),
            P("head", None, ("groups", "seq")),
            P("head", None, ("groups", "seq")),
            P("head", "groups", None),
        ),
        out_specs=P(("groups", "seq"), "head"),
        check_vma=False,
    )
```

```python
import functools

import jax
import jax.numpy as jnp
from jax import lax
from jax.experimental import pallas as pl
from jax.experimental.pallas import tpu as pltpu
from jax.sharding import PartitionSpec as P

DH = 128
BF16 = jnp.bfloat16
F32 = jnp.float32
PARTS = 2
GRANT = 67043328
IN_VMEM = pl.BlockSpec(memory_space=pltpu.VMEM)
IN_HBM = pl.BlockSpec(memory_space=pltpu.HBM)


def split(x):
    high = x.astype(BF16)
    low = (x - high.astype(F32)).astype(BF16)
    return high, low


def beside(x):
    return jnp.concatenate(split(x), axis=1)


def fold_columns(x):
    half = x.shape[1] // 2
    return x[:, :half] + x[:, half:]


def outer_state(k, v):
    full = lax.dot_general(
        beside(k), beside(v), (((0,), (0,)), ((), ())), preferred_element_type=F32
    )
    full = fold_columns(full)
    return full[:DH] + full[DH:]


def through_state(scaled, state):
    wide = beside(state)
    return jnp.dot(
        beside(scaled), jnp.concatenate([wide, wide], axis=0), preferred_element_type=F32
    )


def first_head(place, per):
    own = 1 - lax.rem(lax.axis_index("seq"), 2)
    half = own if place < PARTS else 1 - own
    return (half * PARTS + place % PARTS) * per


def head_columns(head, count=1):
    return pl.ds(pl.multiple_of(head * DH, DH), count * DH)


def given_kernel(place, k_hbm, v_hbm, out_ref, k_buf, v_buf, sems):
    per = out_ref.shape[0]
    columns = head_columns(first_head(place, per), per)
    copies = (
        pltpu.make_async_copy(k_hbm.at[:, columns], k_buf, sems.at[0]),
        pltpu.make_async_copy(v_hbm.at[:, columns], v_buf, sems.at[1]),
    )
    for copy in copies:
        copy.start()
    for copy in copies:
        copy.wait()
    for j in range(per):
        at = slice(j * DH, (j + 1) * DH)
        out_ref[j] = outer_state(k_buf[:, at], v_buf[:, at])


def given_states(keys, values):
    rows, columns = keys.shape
    width = columns // (2 * PARTS)
    return pl.pallas_call(
        functools.partial(given_kernel, PARTS),
        out_shape=jax.ShapeDtypeStruct((width // DH, DH, DH), F32),
        in_specs=[IN_HBM] * 2,
        out_specs=IN_VMEM,
        scratch_shapes=[
            pltpu.VMEM((rows, width), F32),
            pltpu.VMEM((rows, width), F32),
            pltpu.SemaphoreType.DMA((2,)),
        ],
        compiler_params=pltpu.CompilerParams(vmem_limit_bytes=GRANT - 105 * rows * columns * 4 // 10),
        cost_estimate=pl.CostEstimate(
            flops=2 * rows * columns * DH, bytes_accessed=2 * rows * columns, transcendentals=0
        ),
        name="states_given",
    )(keys, values)


def own_kernel(
    levels, buckets, line_ref, q_hbm, k_hbm, v_hbm, prefix_hbm,
    q_out, k_out, v_out, prefix_out, weight_ref, whole_ref, *refs,
):
    (*part_refs, given_ref), sems = refs[:-1], refs[-1]
    per = given_ref.shape[0]
    half = PARTS * per
    copies = []
    for i, (source, to) in enumerate(((k_hbm, k_out), (v_hbm, v_out), (q_hbm, q_out))):
        for h in range(2):
            copy = pltpu.make_async_copy(
                source.at[:, head_columns(first_head(h * PARTS, per), half)],
                to.at[:, h * half * DH : (h + 1) * half * DH],
                sems.at[i, h],
            )
            copy.start()
            copies.append(copy)
    copies.append(
        pltpu.make_async_copy(prefix_hbm.at[pl.ds(first_head(0, per), per)], prefix_out, sems.at[3, 0])
    )
    copies[-1].start()
    position = lax.axis_index("seq")
    own_second = lax.rem(position, 2) == 0
    rows = line_ref.shape[1]
    heads = q_hbm.shape[1] // DH
    lines = []
    for i in range(levels):
        line = line_ref[i * heads : (i + 1) * heads]
        if i:
            line = line * lax.rem(lax.shift_right_logical(position, i - 1), 2).astype(F32)
        lines.append(jnp.where(own_second, jnp.concatenate([line[half:], line[:half]], axis=0), line))
    first = line_ref[heads * levels : heads * levels + half * buckets]
    second = line_ref[heads * levels + half * buckets :]
    lines.append(jnp.where(own_second, second, first))
    lines.append(jnp.where(own_second, first, second))
    spare = weight_ref.shape[1] - heads * (levels + buckets)
    if spare:
        lines.append(jnp.zeros((spare, rows), F32))
    weight_ref[...] = jnp.transpose(jnp.concatenate(lines, axis=0))

    copies[1].wait()
    copies[3].wait()
    for j in range(per):
        head = half + (PARTS - 1) * per + j
        at = slice(head * DH, (head + 1) * DH)
        given_ref[j] = outer_state(k_out[:, at], v_out[:, at])
    copies[0].wait()
    copies[2].wait()
    for c, part_ref in enumerate(part_refs):
        for j in range(per):
            at = slice((c * per + j) * DH, (c * per + j + 1) * DH)
            state = outer_state(k_out[:, at], v_out[:, at])
            part_ref[j] = state
            whole_ref[c * per + j] = state
    for i in (4, 5, 6):
        copies[i].wait()


def own_block_states(queries, keys, values, level_weight, prefix_weight, prefix_state):
    rows, columns = keys.shape
    heads = columns // DH
    per = heads // (2 * PARTS)
    weights = heads * (level_weight.shape[1] + prefix_weight.shape[1])
    lines = jnp.concatenate(
        [
            jnp.transpose(level_weight, (1, 0, 2)).reshape(-1, rows),
            prefix_weight.reshape(-1, rows),
        ],
        axis=0,
    )
    shapes = [queries.shape, keys.shape, values.shape, (per, *prefix_state.shape[1:])]
    shapes += [(rows, pl.cdiv(weights, DH) * DH)]
    shapes += [(PARTS * per, DH, DH)] + [(per, DH, DH)] * (PARTS + 1)
    return pl.pallas_call(
        functools.partial(own_kernel, level_weight.shape[1], prefix_weight.shape[1]),
        out_shape=[jax.ShapeDtypeStruct(s, F32) for s in shapes],
        in_specs=[IN_VMEM] + [IN_HBM] * 4,
        out_specs=[IN_VMEM] * len(shapes),
        scratch_shapes=[pltpu.SemaphoreType.DMA((4, 2))],
        compiler_params=pltpu.CompilerParams(vmem_limit_bytes=GRANT - 153 * rows * columns * 4 // 10),
        cost_estimate=pl.CostEstimate(
            flops=4 * rows * columns * DH, bytes_accessed=24 * rows * columns, transcendentals=0
        ),
        name="states_own",
    )(lines, queries, keys, values, prefix_state)


def base_kernel(place, levels, buckets, q_ref, k_ref, v_ref, weight_ref, prefix_ref, *refs):
    rows = q_ref.shape[0]
    heads = q_ref.shape[1] // DH
    per = prefix_ref.shape[0]
    copy = None
    if len(refs) > 1:
        prefix_hbm, out_ref, next_ref, sem = refs
        following = pl.ds(first_head(place + 1, per), per)
        copy = pltpu.make_async_copy(prefix_hbm.at[following], next_ref, sem)
        copy.start()
    else:
        (out_ref,) = refs
    row = lax.broadcasted_iota(jnp.int32, (rows, rows), 0)
    column = lax.broadcasted_iota(jnp.int32, (rows, rows), 1)
    nt = (((1,), (1,)), ((), ()))
    for j in range(per):
        head = place * per + j
        at = slice(head * DH, (head + 1) * DH)
        q, k, v = q_ref[:, at], k_ref[:, at], v_ref[:, at]
        k_high, k_low = split(k)
        q_wide = beside(q)
        scores = lax.dot_general(
            q_wide, jnp.concatenate([k_high, k_high], axis=1), nt, preferred_element_type=F32
        ) + lax.dot_general(
            q_wide, jnp.concatenate([k_low, k_low], axis=1), nt, preferred_element_type=F32
        )
        scores = jnp.where(column <= row, scores, 0.0) * weight_ref[:, head : head + 1]
        scores_high, scores_low = split(scores)
        v_wide = beside(v)
        total = jnp.dot(scores_high, v_wide, preferred_element_type=F32)
        total += jnp.dot(scores_low, v_wide, preferred_element_type=F32)
        for b in range(buckets):
            line = heads * levels + head * buckets + b
            total += through_state(
                q * weight_ref[:, line : line + 1], prefix_ref[j, b * DH : (b + 1) * DH, :]
            )
        out_ref[:, j * DH : (j + 1) * DH] = fold_columns(total)
    if copy is not None:
        copy.wait()


def base_part(place, levels, buckets, loaded, prefix, prefix_state):
    rows, columns = loaded[0].shape
    per = prefix.shape[0]
    more = place + 1 < 2 * PARTS
    shapes = [(rows, per * DH)] + [prefix.shape] * more
    return pl.pallas_call(
        functools.partial(base_kernel, place, levels, buckets),
        out_shape=[jax.ShapeDtypeStruct(s, F32) for s in shapes],
        in_specs=[IN_VMEM] * (len(loaded) + 1) + [IN_HBM] * more,
        out_specs=[IN_VMEM] * len(shapes),
        scratch_shapes=[pltpu.SemaphoreType.DMA] * more,
        compiler_params=pltpu.CompilerParams(vmem_limit_bytes=GRANT - 17 * rows * columns * 4),
        cost_estimate=pl.CostEstimate(
            flops=2 * per * DH * rows * rows * 24,
            bytes_accessed=20 * rows * per * DH,
            transcendentals=0,
        ),
    )(*loaded, prefix, *[prefix_state] * more)


def levels_kernel(places, first, spread, store, q_ref, weight_ref, *refs):
    count = 1 + max(ref for rows in spread for ref, _ in rows)
    state_refs, refs = refs[:count], refs[count:]
    base_refs, refs = refs[: len(places)], refs[len(places) :]
    per = base_refs[0].shape[1] // DH
    heads = q_ref.shape[1] // DH
    if store:
        out_hbm, buf, sems = refs[-3:]
    copies = []
    for c, place in enumerate(places):
        for j in range(per):
            at = slice(j * DH, (j + 1) * DH)
            head = place * per + j
            q = q_ref[:, head * DH : (head + 1) * DH]
            total = None
            for i, rows in enumerate(spread):
                column = (1 + first + i) * heads + head
                ref, entry = rows[c]
                term = through_state(q * weight_ref[:, column : column + 1], state_refs[ref][entry + j])
                total = term if total is None else total + term
            done = base_refs[c][:, at] + fold_columns(total)
            if store:
                buf[c, :, at] = done
            else:
                refs[c][:, at] = done
        if store:
            columns = head_columns(first_head(place, per), per)
            copy = pltpu.make_async_copy(buf.at[c], out_hbm.at[:, columns], sems.at[c])
            copy.start()
            copies.append(copy)
    for copy in copies:
        copy.wait()


def add_levels(queries, weights, bases, states, spread, places, first, store, out):
    rows, columns = queries.shape
    width = columns // (2 * PARTS)
    count = len(places)
    operands = [queries, weights, *states, *bases]
    in_specs = [IN_VMEM] * len(operands)
    aliases = {}
    if out is not None:
        aliases = {len(operands): 0}
        operands.append(out)
        in_specs.append(IN_HBM)
    shape = (rows, columns) if store else (rows, width)
    return pl.pallas_call(
        functools.partial(levels_kernel, places, first, spread, store),
        out_shape=[jax.ShapeDtypeStruct(shape, F32)] * (1 if store else count),
        in_specs=in_specs,
        out_specs=[IN_HBM if store else IN_VMEM] * (1 if store else count),
        scratch_shapes=[pltpu.VMEM((count, rows, width), F32), pltpu.SemaphoreType.DMA((count,))]
        if store
        else [],
        input_output_aliases=aliases,
        compiler_params=pltpu.CompilerParams(vmem_limit_bytes=GRANT // 4),
        cost_estimate=pl.CostEstimate(
            flops=4 * count * width * rows * rows * len(spread),
            bytes_accessed=12 * rows * width * count,
            transcendentals=0,
        ),
    )(*operands)


def swapped(array, bit, keep=lambda i: True):
    size = lax.axis_size("seq")
    pairs = [(i, i ^ 1 << bit) for i in range(size) if keep(i)]
    return lax.ppermute(array, "seq", pairs)


def attend(queries, keys, values, level_weight, prefix_weight, prefix_state):
    levels = lax.axis_size("seq").bit_length() - 1
    per = queries.shape[1] // DH // (2 * PARTS)
    places = range(PARTS)

    given = [given_states(keys, values)]
    *loaded, prefix, weights, own, part0, part1, rest = own_block_states(
        queries, keys, values, level_weight, prefix_weight, prefix_state
    )
    given.append(rest)
    received = [swapped(given[c], 0) for c in places]
    parts = (part0, part1)
    loaded.append(weights)
    query_places = loaded[0]
    base = []
    for place in range(2 * PARTS):
        done, *following = base_part(place, level_weight.shape[1], prefix_weight.shape[1], loaded, prefix, prefix_state)
        base.append(done)
        if following:
            (prefix,) = following

    own_states = [list(received)]
    running = [parts[c] + received[c] for c in places]
    for bit in range(1, levels):
        arrived = [swapped(running[c], bit) for c in places]
        own_states.append(arrived)
        running = [a + b for a, b in zip(running, arrived)]
    other_states = [[swapped(own, 0)]]
    for bit in range(1, levels - 1):
        both = jnp.concatenate(own_states[bit], axis=0)
        other_states.append([swapped(both, 0)])
    top = levels - 1
    needs = lambda i: i >> top & 1
    last = [swapped(own_states[top][c], 0, needs if c == PARTS - 1 else lambda i: True) for c in places]

    spread = [[(i, c * per) for c in places] for i in range(levels - 1)]
    middle = add_levels(
        query_places, weights, base[PARTS:], [x[0] for x in other_states], spread, (2, 3), 0, False, None
    )
    flat = [x for level in own_states for x in level]
    spread = [[(i * PARTS + c, 0) for c in places] for i in range(levels)]
    (out,) = add_levels(query_places, weights, base[:PARTS], flat, spread, (0, 1), 0, True, None)
    for c in places:
        (out,) = add_levels(query_places, weights, [middle[c]], [last[c]], [[(0, 0)]], (PARTS + c,), top, True, out)
    return out


def solution(mesh):
    return jax.shard_map(
        attend,
        mesh=mesh,
        in_specs=(
            P(("groups", "seq"), "head"),
            P(("groups", "seq"), "head"),
            P(("groups", "seq"), "head"),
            P("head", None, ("groups", "seq")),
            P("head", None, ("groups", "seq")),
            P("head", "groups", None),
        ),
        out_specs=P(("groups", "seq"), "head"),
        check_vma=False,
    )
```

```python
import functools

import jax
import jax.numpy as jnp
from jax import lax
from jax.experimental import pallas as pl
from jax.experimental.pallas import tpu as pltpu
from jax.sharding import PartitionSpec as P

DH = 128
BF16 = jnp.bfloat16
F32 = jnp.float32
PARTS = 2
GRANT = 67043328
IN_VMEM = pl.BlockSpec(memory_space=pltpu.VMEM)
IN_HBM = pl.BlockSpec(memory_space=pltpu.HBM)


def split(x):
    high = x.astype(BF16)
    low = (x - high.astype(F32)).astype(BF16)
    return high, low


def beside(x):
    return jnp.concatenate(split(x), axis=1)


def fold_columns(x):
    half = x.shape[1] // 2
    return x[:, :half] + x[:, half:]


def outer_state(k, v):
    full = lax.dot_general(
        beside(k), beside(v), (((0,), (0,)), ((), ())), preferred_element_type=F32
    )
    full = fold_columns(full)
    return full[:DH] + full[DH:]


def through_state(scaled, state):
    wide = beside(state)
    return jnp.dot(
        beside(scaled), jnp.concatenate([wide, wide], axis=0), preferred_element_type=F32
    )


def first_head(place, per):
    own = 1 - lax.rem(lax.axis_index("seq"), 2)
    half = own if place < PARTS else 1 - own
    return (half * PARTS + place % PARTS) * per


def head_columns(head, count=1):
    return pl.ds(pl.multiple_of(head * DH, DH), count * DH)


def given_kernel(place, k_hbm, v_hbm, out_ref, k_buf, v_buf, sems):
    per = out_ref.shape[0]
    columns = head_columns(first_head(place, per), per)
    copies = (
        pltpu.make_async_copy(k_hbm.at[:, columns], k_buf, sems.at[0]),
        pltpu.make_async_copy(v_hbm.at[:, columns], v_buf, sems.at[1]),
    )
    for copy in copies:
        copy.start()
    for copy in copies:
        copy.wait()
    for j in range(per):
        at = slice(j * DH, (j + 1) * DH)
        out_ref[j] = outer_state(k_buf[:, at], v_buf[:, at])


def given_states(keys, values):
    rows, columns = keys.shape
    width = columns // (2 * PARTS)
    return pl.pallas_call(
        functools.partial(given_kernel, PARTS),
        out_shape=jax.ShapeDtypeStruct((width // DH, DH, DH), F32),
        in_specs=[IN_HBM] * 2,
        out_specs=IN_VMEM,
        scratch_shapes=[
            pltpu.VMEM((rows, width), F32),
            pltpu.VMEM((rows, width), F32),
            pltpu.SemaphoreType.DMA((2,)),
        ],
        compiler_params=pltpu.CompilerParams(vmem_limit_bytes=GRANT - 105 * rows * columns * 4 // 10),
        cost_estimate=pl.CostEstimate(
            flops=2 * rows * columns * DH, bytes_accessed=2 * rows * columns, transcendentals=0
        ),
        name="states_given",
    )(keys, values)


def own_kernel(
    levels, buckets, line_ref, q_hbm, k_hbm, v_hbm, prefix_hbm,
    q_out, k_out, v_out, prefix_out, weight_ref, whole_ref, *refs,
):
    (*part_refs, given_ref), sems = refs[:-1], refs[-1]
    per = given_ref.shape[0]
    half = PARTS * per
    copies = []
    for i, (source, to) in enumerate(((k_hbm, k_out), (v_hbm, v_out), (q_hbm, q_out))):
        for h in range(2):
            copy = pltpu.make_async_copy(
                source.at[:, head_columns(first_head(h * PARTS, per), half)],
                to.at[:, h * half * DH : (h + 1) * half * DH],
                sems.at[i, h],
            )
            copy.start()
            copies.append(copy)
    copies.append(
        pltpu.make_async_copy(prefix_hbm.at[pl.ds(first_head(0, per), per)], prefix_out, sems.at[3, 0])
    )
    copies[-1].start()
    position = lax.axis_index("seq")
    own_second = lax.rem(position, 2) == 0
    rows = line_ref.shape[1]
    heads = q_hbm.shape[1] // DH
    lines = []
    for i in range(levels):
        line = line_ref[i * heads : (i + 1) * heads]
        if i:
            line = line * lax.rem(lax.shift_right_logical(position, i - 1), 2).astype(F32)
        lines.append(jnp.where(own_second, jnp.concatenate([line[half:], line[:half]], axis=0), line))
    first = line_ref[heads * levels : heads * levels + half * buckets]
    second = line_ref[heads * levels + half * buckets :]
    lines.append(jnp.where(own_second, second, first))
    lines.append(jnp.where(own_second, first, second))
    spare = weight_ref.shape[1] - heads * (levels + buckets)
    if spare:
        lines.append(jnp.zeros((spare, rows), F32))
    weight_ref[...] = jnp.transpose(jnp.concatenate(lines, axis=0))

    copies[1].wait()
    copies[3].wait()
    for j in range(per):
        head = half + (PARTS - 1) * per + j
        at = slice(head * DH, (head + 1) * DH)
        given_ref[j] = outer_state(k_out[:, at], v_out[:, at])
    copies[0].wait()
    copies[2].wait()
    for c, part_ref in enumerate(part_refs):
        for j in range(per):
            at = slice((c * per + j) * DH, (c * per + j + 1) * DH)
            state = outer_state(k_out[:, at], v_out[:, at])
            part_ref[j] = state
            whole_ref[c * per + j] = state
    for i in (4, 5, 6):
        copies[i].wait()


def own_block_states(queries, keys, values, level_weight, prefix_weight, prefix_state):
    rows, columns = keys.shape
    heads = columns // DH
    per = heads // (2 * PARTS)
    weights = heads * (level_weight.shape[1] + prefix_weight.shape[1])
    lines = jnp.concatenate(
        [
            jnp.transpose(level_weight, (1, 0, 2)).reshape(-1, rows),
            prefix_weight.reshape(-1, rows),
        ],
        axis=0,
    )
    shapes = [queries.shape, keys.shape, values.shape, (per, *prefix_state.shape[1:])]
    shapes += [(rows, pl.cdiv(weights, DH) * DH)]
    shapes += [(PARTS * per, DH, DH)] + [(per, DH, DH)] * (PARTS + 1)
    return pl.pallas_call(
        functools.partial(own_kernel, level_weight.shape[1], prefix_weight.shape[1]),
        out_shape=[jax.ShapeDtypeStruct(s, F32) for s in shapes],
        in_specs=[IN_VMEM] + [IN_HBM] * 4,
        out_specs=[IN_VMEM] * len(shapes),
        scratch_shapes=[pltpu.SemaphoreType.DMA((4, 2))],
        compiler_params=pltpu.CompilerParams(vmem_limit_bytes=GRANT - 153 * rows * columns * 4 // 10),
        cost_estimate=pl.CostEstimate(
            flops=4 * rows * columns * DH, bytes_accessed=24 * rows * columns, transcendentals=0
        ),
        name="states_own",
    )(lines, queries, keys, values, prefix_state)


def base_kernel(place, levels, buckets, q_ref, k_ref, v_ref, weight_ref, prefix_ref, *refs):
    rows = q_ref.shape[0]
    heads = q_ref.shape[1] // DH
    per = prefix_ref.shape[0]
    copy = None
    if len(refs) > 1:
        prefix_hbm, out_ref, next_ref, sem = refs
        following = pl.ds(first_head(place + 1, per), per)
        copy = pltpu.make_async_copy(prefix_hbm.at[following], next_ref, sem)
        copy.start()
    else:
        (out_ref,) = refs
    row = lax.broadcasted_iota(jnp.int32, (rows, rows), 0)
    column = lax.broadcasted_iota(jnp.int32, (rows, rows), 1)
    nt = (((1,), (1,)), ((), ()))
    for j in range(per):
        head = place * per + j
        at = slice(head * DH, (head + 1) * DH)
        q, k, v = q_ref[:, at], k_ref[:, at], v_ref[:, at]
        k_high, k_low = split(k)
        q_wide = beside(q)
        scores = lax.dot_general(
            q_wide, jnp.concatenate([k_high, k_high], axis=1), nt, preferred_element_type=F32
        ) + lax.dot_general(
            q_wide, jnp.concatenate([k_low, k_low], axis=1), nt, preferred_element_type=F32
        )
        scores = jnp.where(column <= row, scores, 0.0) * weight_ref[:, head : head + 1]
        scores_high, scores_low = split(scores)
        v_wide = beside(v)
        total = jnp.dot(scores_high, v_wide, preferred_element_type=F32)
        total += jnp.dot(scores_low, v_wide, preferred_element_type=F32)
        for b in range(buckets):
            line = heads * levels + head * buckets + b
            total += through_state(
                q * weight_ref[:, line : line + 1], prefix_ref[j, b * DH : (b + 1) * DH, :]
            )
        out_ref[:, j * DH : (j + 1) * DH] = fold_columns(total)
    if copy is not None:
        copy.wait()


def base_part(place, levels, buckets, loaded, prefix, prefix_state):
    rows, columns = loaded[0].shape
    per = prefix.shape[0]
    more = place + 1 < 2 * PARTS
    shapes = [(rows, per * DH)] + [prefix.shape] * more
    return pl.pallas_call(
        functools.partial(base_kernel, place, levels, buckets),
        out_shape=[jax.ShapeDtypeStruct(s, F32) for s in shapes],
        in_specs=[IN_VMEM] * (len(loaded) + 1) + [IN_HBM] * more,
        out_specs=[IN_VMEM] * len(shapes),
        scratch_shapes=[pltpu.SemaphoreType.DMA] * more,
        compiler_params=pltpu.CompilerParams(vmem_limit_bytes=GRANT - 17 * rows * columns * 4),
        cost_estimate=pl.CostEstimate(
            flops=2 * per * DH * rows * rows * 24,
            bytes_accessed=20 * rows * per * DH,
            transcendentals=0,
        ),
    )(*loaded, prefix, *[prefix_state] * more)


def levels_kernel(places, terms, states, store, q_ref, weight_ref, *refs):
    state_refs, refs = refs[:states], refs[states:]
    base_refs, refs = refs[: len(places)], refs[len(places) :]
    per = base_refs[0].shape[1] // DH
    heads = q_ref.shape[1] // DH
    if store:
        out_hbm, buf, sems = refs[-3:]
    copies = []
    for c, place in enumerate(places):
        for j in range(per):
            at = slice(j * DH, (j + 1) * DH)
            head = place * per + j
            q = q_ref[:, head * DH : (head + 1) * DH]
            total = None
            for level, ref, entry in terms[c]:
                column = level * heads + head
                term = through_state(q * weight_ref[:, column : column + 1], state_refs[ref][entry + j])
                total = term if total is None else total + term
            done = base_refs[c][:, at]
            if total is not None:
                done += fold_columns(total)
            if store:
                buf[c, :, at] = done
            else:
                refs[c][:, at] = done
        if store:
            columns = head_columns(first_head(place, per), per)
            copy = pltpu.make_async_copy(buf.at[c], out_hbm.at[:, columns], sems.at[c])
            copy.start()
            copies.append(copy)
    for copy in copies:
        copy.wait()


def add_levels(queries, weights, bases, states, terms, places, store, out):
    rows, columns = queries.shape
    width = columns // (2 * PARTS)
    count = len(places)
    operands = [queries, weights, *states, *bases]
    in_specs = [IN_VMEM] * len(operands)
    aliases = {}
    if out is not None:
        aliases = {len(operands): 0}
        operands.append(out)
        in_specs.append(IN_HBM)
    shape = (rows, columns) if store else (rows, width)
    return pl.pallas_call(
        functools.partial(levels_kernel, places, terms, len(states), store),
        out_shape=[jax.ShapeDtypeStruct(shape, F32)] * (1 if store else count),
        in_specs=in_specs,
        out_specs=[IN_HBM if store else IN_VMEM] * (1 if store else count),
        scratch_shapes=[pltpu.VMEM((count, rows, width), F32), pltpu.SemaphoreType.DMA((count,))]
        if store
        else [],
        input_output_aliases=aliases,
        compiler_params=pltpu.CompilerParams(vmem_limit_bytes=GRANT // 4),
        cost_estimate=pl.CostEstimate(
            flops=4 * width * rows * rows * sum(len(t) for t in terms),
            bytes_accessed=12 * rows * width * count,
            transcendentals=0,
        ),
    )(*operands)


def swapped(array, bit, keep=lambda i: True, alt=None):
    size = lax.axis_size("seq")
    pairs = [(i, i ^ (1 << bit if alt is None or i >> alt & 1 else 2)) for i in range(size) if keep(i)]
    return lax.ppermute(array, "seq", pairs)


def attend(queries, keys, values, level_weight, prefix_weight, prefix_state):
    levels = lax.axis_size("seq").bit_length() - 1
    per = queries.shape[1] // DH // (2 * PARTS)
    places = range(PARTS)

    given = [given_states(keys, values)]
    *loaded, prefix, weights, own, part0, part1, rest = own_block_states(
        queries, keys, values, level_weight, prefix_weight, prefix_state
    )
    given.append(rest)
    received = [swapped(given[c], 0) for c in places]
    parts = (part0, part1)
    loaded.append(weights)
    query_places = loaded[0]
    base = []
    for place in range(2 * PARTS):
        done, *following = base_part(place, level_weight.shape[1], prefix_weight.shape[1], loaded, prefix, prefix_state)
        base.append(done)
        if following:
            (prefix,) = following

    own_states = [list(received)]
    running = [parts[c] + received[c] for c in places]
    for bit in range(1, levels):
        arrived = [swapped(running[c], bit) for c in places]
        own_states.append(arrived)
        running = [a + b for a, b in zip(running, arrived)]
    other_states = [[swapped(own, 0)]]
    for bit in range(1, levels - 1):
        both = jnp.concatenate(own_states[bit], axis=0)
        other_states.append([swapped(both, 0)])
    top = levels - 1
    needs = lambda i: i >> top & 1
    last = [swapped(own_states[top][c], 0, needs if c == PARTS - 1 else lambda i: True, top) for c in places]

    flat = [x for level in own_states for x in level]
    terms = [[(1 + i, i * PARTS + c, 0) for i in range(levels)] for c in places]
    (out,) = add_levels(query_places, weights, base[:PARTS], flat, terms, tuple(places), True, None)
    flat = [x[0] for x in other_states] + last[:-1]
    terms = [[(1 + i, i, c * per) for i in range(levels - 1)] for c in places]
    for c in places[:-1]:
        terms[c].append((levels, levels - 1 + c, 0))
    other = tuple(PARTS + c for c in places)
    middle = add_levels(query_places, weights, base[PARTS:], flat, terms, other, False, None)
    terms = [[] for _ in places[:-1]] + [[(levels, 0, 0)]]
    (out,) = add_levels(query_places, weights, middle, last[-1:], terms, other, True, out)
    return out


def solution(mesh):
    return jax.shard_map(
        attend,
        mesh=mesh,
        in_specs=(
            P(("groups", "seq"), "head"),
            P(("groups", "seq"), "head"),
            P(("groups", "seq"), "head"),
            P("head", None, ("groups", "seq")),
            P("head", None, ("groups", "seq")),
            P("head", "groups", None),
        ),
        out_specs=P(("groups", "seq"), "head"),
        check_vma=False,
    )
```

```python
import functools

import jax
import jax.numpy as jnp
from jax import lax
from jax.experimental import pallas as pl
from jax.experimental.pallas import tpu as pltpu
from jax.sharding import PartitionSpec as P

DH = 128
BF16 = jnp.bfloat16
F32 = jnp.float32
PARTS = 2
GRANT = 67043328
IN_VMEM = pl.BlockSpec(memory_space=pltpu.VMEM)
IN_HBM = pl.BlockSpec(memory_space=pltpu.HBM)


def split(x):
    high = x.astype(BF16)
    low = (x - high.astype(F32)).astype(BF16)
    return high, low


def beside(x):
    return jnp.concatenate(split(x), axis=1)


def fold_columns(x):
    half = x.shape[1] // 2
    return x[:, :half] + x[:, half:]


def outer_state(k, v):
    full = lax.dot_general(
        beside(k), beside(v), (((0,), (0,)), ((), ())), preferred_element_type=F32
    )
    full = fold_columns(full)
    return full[:DH] + full[DH:]


def through_state(scaled, state):
    wide = beside(state)
    return jnp.dot(
        beside(scaled), jnp.concatenate([wide, wide], axis=0), preferred_element_type=F32
    )


def first_head(place, per):
    own = 1 - lax.rem(lax.axis_index("seq"), 2)
    half = own if place < PARTS else 1 - own
    return (half * PARTS + place % PARTS) * per


def head_columns(head, count=1):
    return pl.ds(pl.multiple_of(head * DH, DH), count * DH)


def given_kernel(place, k_hbm, v_hbm, out_ref, k_buf, v_buf, sems):
    per = out_ref.shape[0]
    columns = head_columns(first_head(place, per), per)
    copies = (
        pltpu.make_async_copy(k_hbm.at[:, columns], k_buf, sems.at[0]),
        pltpu.make_async_copy(v_hbm.at[:, columns], v_buf, sems.at[1]),
    )
    for copy in copies:
        copy.start()
    for copy in copies:
        copy.wait()
    for j in range(per):
        at = slice(j * DH, (j + 1) * DH)
        out_ref[j] = outer_state(k_buf[:, at], v_buf[:, at])


def given_states(keys, values):
    rows, columns = keys.shape
    width = columns // (2 * PARTS)
    return pl.pallas_call(
        functools.partial(given_kernel, PARTS),
        out_shape=jax.ShapeDtypeStruct((width // DH, DH, DH), F32),
        in_specs=[IN_HBM] * 2,
        out_specs=IN_VMEM,
        scratch_shapes=[
            pltpu.VMEM((rows, width), F32),
            pltpu.VMEM((rows, width), F32),
            pltpu.SemaphoreType.DMA((2,)),
        ],
        compiler_params=pltpu.CompilerParams(vmem_limit_bytes=GRANT - 105 * rows * columns * 4 // 10),
        cost_estimate=pl.CostEstimate(
            flops=2 * rows * columns * DH, bytes_accessed=2 * rows * columns, transcendentals=0
        ),
        name="states_given",
    )(keys, values)


def own_kernel(
    levels, buckets, line_ref, q_hbm, k_hbm, v_hbm, prefix_hbm,
    q_out, k_out, v_out, prefix_out, weight_ref, whole_ref, *refs,
):
    (*part_refs, given_ref), sems = refs[:-1], refs[-1]
    per = given_ref.shape[0]
    half = PARTS * per
    copies = []
    for i, (source, to) in enumerate(((k_hbm, k_out), (v_hbm, v_out), (q_hbm, q_out))):
        for h in range(2):
            copy = pltpu.make_async_copy(
                source.at[:, head_columns(first_head(h * PARTS, per), half)],
                to.at[:, h * half * DH : (h + 1) * half * DH],
                sems.at[i, h],
            )
            copy.start()
            copies.append(copy)
    copies.append(
        pltpu.make_async_copy(prefix_hbm.at[pl.ds(first_head(0, per), per)], prefix_out, sems.at[3, 0])
    )
    copies[-1].start()
    position = lax.axis_index("seq")
    own_second = lax.rem(position, 2) == 0
    rows = line_ref.shape[1]
    heads = q_hbm.shape[1] // DH
    lines = []
    for i in range(levels):
        line = line_ref[i * heads : (i + 1) * heads]
        if i:
            line = line * lax.rem(lax.shift_right_logical(position, i - 1), 2).astype(F32)
        lines.append(jnp.where(own_second, jnp.concatenate([line[half:], line[:half]], axis=0), line))
    first = line_ref[heads * levels : heads * levels + half * buckets]
    second = line_ref[heads * levels + half * buckets :]
    lines.append(jnp.where(own_second, second, first))
    lines.append(jnp.where(own_second, first, second))
    spare = weight_ref.shape[1] - heads * (levels + buckets)
    if spare:
        lines.append(jnp.zeros((spare, rows), F32))
    weight_ref[...] = jnp.transpose(jnp.concatenate(lines, axis=0))

    copies[1].wait()
    copies[3].wait()
    for j in range(per):
        head = half + (PARTS - 1) * per + j
        at = slice(head * DH, (head + 1) * DH)
        given_ref[j] = outer_state(k_out[:, at], v_out[:, at])
    copies[0].wait()
    copies[2].wait()
    for c, part_ref in enumerate(part_refs):
        for j in range(per):
            at = slice((c * per + j) * DH, (c * per + j + 1) * DH)
            state = outer_state(k_out[:, at], v_out[:, at])
            part_ref[j] = state
            whole_ref[c * per + j] = state
    for i in (4, 5, 6):
        copies[i].wait()


def own_block_states(queries, keys, values, level_weight, prefix_weight, prefix_state):
    rows, columns = keys.shape
    heads = columns // DH
    per = heads // (2 * PARTS)
    weights = heads * (level_weight.shape[1] + prefix_weight.shape[1])
    lines = jnp.concatenate(
        [
            jnp.transpose(level_weight, (1, 0, 2)).reshape(-1, rows),
            prefix_weight.reshape(-1, rows),
        ],
        axis=0,
    )
    shapes = [queries.shape, keys.shape, values.shape, (per, *prefix_state.shape[1:])]
    shapes += [(rows, pl.cdiv(weights, DH) * DH)]
    shapes += [(PARTS * per, DH, DH)] + [(per, DH, DH)] * (PARTS + 1)
    return pl.pallas_call(
        functools.partial(own_kernel, level_weight.shape[1], prefix_weight.shape[1]),
        out_shape=[jax.ShapeDtypeStruct(s, F32) for s in shapes],
        in_specs=[IN_VMEM] + [IN_HBM] * 4,
        out_specs=[IN_VMEM] * len(shapes),
        scratch_shapes=[pltpu.SemaphoreType.DMA((4, 2))],
        compiler_params=pltpu.CompilerParams(vmem_limit_bytes=GRANT - 153 * rows * columns * 4 // 10),
        cost_estimate=pl.CostEstimate(
            flops=4 * rows * columns * DH, bytes_accessed=24 * rows * columns, transcendentals=0
        ),
        name="states_own",
    )(lines, queries, keys, values, prefix_state)


def base_kernel(place, levels, buckets, q_ref, k_ref, v_ref, weight_ref, prefix_ref, *refs):
    rows = q_ref.shape[0]
    heads = q_ref.shape[1] // DH
    per = prefix_ref.shape[0]
    copy = None
    if len(refs) > 1:
        prefix_hbm, out_ref, next_ref, sem = refs
        following = pl.ds(first_head(place + 1, per), per)
        copy = pltpu.make_async_copy(prefix_hbm.at[following], next_ref, sem)
        copy.start()
    else:
        (out_ref,) = refs
    row = lax.broadcasted_iota(jnp.int32, (rows, rows), 0)
    column = lax.broadcasted_iota(jnp.int32, (rows, rows), 1)
    nt = (((1,), (1,)), ((), ()))
    for j in range(per):
        head = place * per + j
        at = slice(head * DH, (head + 1) * DH)
        q, k, v = q_ref[:, at], k_ref[:, at], v_ref[:, at]
        k_high, k_low = split(k)
        q_wide = beside(q)
        scores = lax.dot_general(
            q_wide, jnp.concatenate([k_high, k_high], axis=1), nt, preferred_element_type=F32
        ) + lax.dot_general(
            q_wide, jnp.concatenate([k_low, k_low], axis=1), nt, preferred_element_type=F32
        )
        scores = jnp.where(column <= row, scores, 0.0) * weight_ref[:, head : head + 1]
        scores_high, scores_low = split(scores)
        v_wide = beside(v)
        total = jnp.dot(scores_high, v_wide, preferred_element_type=F32)
        total += jnp.dot(scores_low, v_wide, preferred_element_type=F32)
        for b in range(buckets):
            line = heads * levels + head * buckets + b
            total += through_state(
                q * weight_ref[:, line : line + 1], prefix_ref[j, b * DH : (b + 1) * DH, :]
            )
        out_ref[:, j * DH : (j + 1) * DH] = fold_columns(total)
    if copy is not None:
        copy.wait()


def base_part(place, levels, buckets, loaded, prefix, prefix_state):
    rows, columns = loaded[0].shape
    per = prefix.shape[0]
    more = place + 1 < 2 * PARTS
    shapes = [(rows, per * DH)] + [prefix.shape] * more
    return pl.pallas_call(
        functools.partial(base_kernel, place, levels, buckets),
        out_shape=[jax.ShapeDtypeStruct(s, F32) for s in shapes],
        in_specs=[IN_VMEM] * (len(loaded) + 1) + [IN_HBM] * more,
        out_specs=[IN_VMEM] * len(shapes),
        scratch_shapes=[pltpu.SemaphoreType.DMA] * more,
        compiler_params=pltpu.CompilerParams(vmem_limit_bytes=GRANT - 17 * rows * columns * 4),
        cost_estimate=pl.CostEstimate(
            flops=2 * per * DH * rows * rows * 24,
            bytes_accessed=20 * rows * per * DH,
            transcendentals=0,
        ),
    )(*loaded, prefix, *[prefix_state] * more)


def levels_kernel(places, terms, states, store, q_ref, weight_ref, *refs):
    state_refs, refs = refs[:states], refs[states:]
    base_refs, refs = refs[: len(places)], refs[len(places) :]
    per = base_refs[0].shape[1] // DH
    heads = q_ref.shape[1] // DH
    if store:
        out_hbm, buf, sems = refs[-3:]
    copies = []
    for c, place in enumerate(places):
        for j in range(per):
            at = slice(j * DH, (j + 1) * DH)
            head = place * per + j
            q = q_ref[:, head * DH : (head + 1) * DH]
            total = None
            for level, ref, entry in terms[c]:
                column = level * heads + head
                term = through_state(q * weight_ref[:, column : column + 1], state_refs[ref][entry + j])
                total = term if total is None else total + term
            done = base_refs[c][:, at]
            if total is not None:
                done += fold_columns(total)
            if store:
                buf[c, :, at] = done
            else:
                refs[c][:, at] = done
        if store:
            columns = head_columns(first_head(place, per), per)
            copy = pltpu.make_async_copy(buf.at[c], out_hbm.at[:, columns], sems.at[c])
            copy.start()
            copies.append(copy)
    for copy in copies:
        copy.wait()


def add_levels(queries, weights, bases, states, terms, places, store, out):
    rows, columns = queries.shape
    width = columns // (2 * PARTS)
    count = len(places)
    operands = [queries, weights, *states, *bases]
    in_specs = [IN_VMEM] * len(operands)
    aliases = {}
    if out is not None:
        aliases = {len(operands): 0}
        operands.append(out)
        in_specs.append(IN_HBM)
    shape = (rows, columns) if store else (rows, width)
    return pl.pallas_call(
        functools.partial(levels_kernel, places, terms, len(states), store),
        out_shape=[jax.ShapeDtypeStruct(shape, F32)] * (1 if store else count),
        in_specs=in_specs,
        out_specs=[IN_HBM if store else IN_VMEM] * (1 if store else count),
        scratch_shapes=[pltpu.VMEM((count, rows, width), F32), pltpu.SemaphoreType.DMA((count,))]
        if store
        else [],
        input_output_aliases=aliases,
        compiler_params=pltpu.CompilerParams(vmem_limit_bytes=GRANT // 4),
        cost_estimate=pl.CostEstimate(
            flops=4 * width * rows * rows * sum(len(t) for t in terms),
            bytes_accessed=12 * rows * width * count,
            transcendentals=0,
        ),
    )(*operands)


def swapped(array, bit, needs=None):
    size, cores = lax.axis_size("seq"), lax.axis_size("head")
    pairs = []
    for i in range(size):
        for core in range(cores):
            if needs is None or needs(i) or cores % 2:
                to = (i ^ 1 << bit) * cores + core
            else:
                to = i * cores + (core ^ 1)
            pairs.append((i * cores + core, to))
    return lax.ppermute(array, ("seq", "head"), pairs)


def attend(queries, keys, values, level_weight, prefix_weight, prefix_state):
    levels = lax.axis_size("seq").bit_length() - 1
    per = queries.shape[1] // DH // (2 * PARTS)
    places = range(PARTS)

    given = [given_states(keys, values)]
    *loaded, prefix, weights, own, part0, part1, rest = own_block_states(
        queries, keys, values, level_weight, prefix_weight, prefix_state
    )
    given.append(rest)
    received = [swapped(given[c], 0) for c in places]
    parts = (part0, part1)
    loaded.append(weights)
    query_places = loaded[0]
    base = []
    for place in range(2 * PARTS):
        done, *following = base_part(place, level_weight.shape[1], prefix_weight.shape[1], loaded, prefix, prefix_state)
        base.append(done)
        if following:
            (prefix,) = following

    own_states = [list(received)]
    running = [parts[c] + received[c] for c in places]
    for bit in range(1, levels):
        arrived = [swapped(running[c], bit) for c in places]
        own_states.append(arrived)
        running = [a + b for a, b in zip(running, arrived)]
    other_states = [[swapped(own, 0)]]
    for bit in range(1, levels - 1):
        both = jnp.concatenate(own_states[bit], axis=0)
        other_states.append([swapped(both, 0)])
    top = levels - 1
    needs = lambda i: i >> top & 1
    last = [swapped(own_states[top][c], 0, needs if c in (0, 1) else None) for c in places]

    flat = [x for level in own_states for x in level]
    terms = [[(1 + i, i * PARTS + c, 0) for i in range(levels)] for c in places]
    (out,) = add_levels(query_places, weights, base[:PARTS], flat, terms, tuple(places), True, None)
    flat = [x[0] for x in other_states] + last[:-1]
    terms = [[(1 + i, i, c * per) for i in range(levels - 1)] for c in places]
    for c in places[:-1]:
        terms[c].append((levels, levels - 1 + c, 0))
    other = tuple(PARTS + c for c in places)
    middle = add_levels(query_places, weights, base[PARTS:], flat, terms, other, False, None)
    terms = [[] for _ in places[:-1]] + [[(levels, 0, 0)]]
    (out,) = add_levels(query_places, weights, middle, last[-1:], terms, other, True, out)
    return out


def solution(mesh):
    return jax.shard_map(
        attend,
        mesh=mesh,
        in_specs=(
            P(("groups", "seq"), "head"),
            P(("groups", "seq"), "head"),
            P(("groups", "seq"), "head"),
            P("head", None, ("groups", "seq")),
            P("head", None, ("groups", "seq")),
            P("head", "groups", None),
        ),
        out_specs=P(("groups", "seq"), "head"),
        check_vma=False,
    )
```

```python
import functools

import jax
import jax.numpy as jnp
from jax import lax
from jax.experimental import pallas as pl
from jax.experimental.pallas import tpu as pltpu
from jax.sharding import PartitionSpec as P

DH = 128
BF16 = jnp.bfloat16
F32 = jnp.float32
PARTS = 2
GRANT = 67043328
IN_VMEM = pl.BlockSpec(memory_space=pltpu.VMEM)
IN_HBM = pl.BlockSpec(memory_space=pltpu.HBM)


def split(x):
    high = x.astype(BF16)
    low = (x - high.astype(F32)).astype(BF16)
    return high, low


def beside(x):
    return jnp.concatenate(split(x), axis=1)


def fold_columns(x):
    half = x.shape[1] // 2
    return x[:, :half] + x[:, half:]


def outer_state(k, v):
    full = lax.dot_general(
        beside(k), beside(v), (((0,), (0,)), ((), ())), preferred_element_type=F32
    )
    full = fold_columns(full)
    return full[:DH] + full[DH:]


def through_state(scaled, state):
    wide = beside(state)
    return jnp.dot(
        beside(scaled), jnp.concatenate([wide, wide], axis=0), preferred_element_type=F32
    )


def first_head(place, per):
    own = 1 - lax.rem(lax.axis_index("seq"), 2)
    half = own if place < PARTS else 1 - own
    return (half * PARTS + place % PARTS) * per


def head_columns(head, count=1):
    return pl.ds(pl.multiple_of(head * DH, DH), count * DH)


def given_kernel(place, k_hbm, v_hbm, out_ref, k_buf, v_buf, sems):
    per = out_ref.shape[0]
    columns = head_columns(first_head(place, per), per)
    copies = (
        pltpu.make_async_copy(k_hbm.at[:, columns], k_buf, sems.at[0]),
        pltpu.make_async_copy(v_hbm.at[:, columns], v_buf, sems.at[1]),
    )
    for copy in copies:
        copy.start()
    for copy in copies:
        copy.wait()
    for j in range(per):
        at = slice(j * DH, (j + 1) * DH)
        out_ref[j] = outer_state(k_buf[:, at], v_buf[:, at])


def given_states(keys, values):
    rows, columns = keys.shape
    width = columns // (2 * PARTS)
    return pl.pallas_call(
        functools.partial(given_kernel, PARTS),
        out_shape=jax.ShapeDtypeStruct((width // DH, DH, DH), F32),
        in_specs=[IN_HBM] * 2,
        out_specs=IN_VMEM,
        scratch_shapes=[
            pltpu.VMEM((rows, width), F32),
            pltpu.VMEM((rows, width), F32),
            pltpu.SemaphoreType.DMA((2,)),
        ],
        compiler_params=pltpu.CompilerParams(vmem_limit_bytes=GRANT - 105 * rows * columns * 4 // 10),
        cost_estimate=pl.CostEstimate(
            flops=2 * rows * columns * DH, bytes_accessed=2 * rows * columns, transcendentals=0
        ),
        name="states_given",
    )(keys, values)


def own_kernel(
    q_hbm, k_hbm, v_hbm, prefix_hbm,
    q_out, k_out, v_out, prefix_out, whole_ref, *refs,
):
    (*part_refs, given_ref), sems = refs[:-1], refs[-1]
    per = given_ref.shape[0]
    half = PARTS * per
    copies = []
    for i, (source, to) in enumerate(((k_hbm, k_out), (v_hbm, v_out), (q_hbm, q_out))):
        for h in range(2):
            copy = pltpu.make_async_copy(
                source.at[:, head_columns(first_head(h * PARTS, per), half)],
                to.at[:, h * half * DH : (h + 1) * half * DH],
                sems.at[i, h],
            )
            copy.start()
            copies.append(copy)
    copies.append(
        pltpu.make_async_copy(prefix_hbm.at[pl.ds(first_head(0, per), per)], prefix_out, sems.at[3, 0])
    )
    copies[-1].start()
    copies[1].wait()
    copies[3].wait()
    for j in range(per):
        head = half + (PARTS - 1) * per + j
        at = slice(head * DH, (head + 1) * DH)
        given_ref[j] = outer_state(k_out[:, at], v_out[:, at])
    copies[0].wait()
    copies[2].wait()
    for c, part_ref in enumerate(part_refs):
        for j in range(per):
            at = slice((c * per + j) * DH, (c * per + j + 1) * DH)
            state = outer_state(k_out[:, at], v_out[:, at])
            part_ref[j] = state
            whole_ref[c * per + j] = state
    for i in (4, 5, 6):
        copies[i].wait()


def own_block_states(queries, keys, values, prefix_state):
    rows, columns = keys.shape
    heads = columns // DH
    per = heads // (2 * PARTS)
    shapes = [queries.shape, keys.shape, values.shape, (per, *prefix_state.shape[1:])]
    shapes += [(PARTS * per, DH, DH)] + [(per, DH, DH)] * (PARTS + 1)
    return pl.pallas_call(
        own_kernel,
        out_shape=[jax.ShapeDtypeStruct(s, F32) for s in shapes],
        in_specs=[IN_HBM] * 4,
        out_specs=[IN_VMEM] * len(shapes),
        scratch_shapes=[pltpu.SemaphoreType.DMA((4, 2))],
        compiler_params=pltpu.CompilerParams(vmem_limit_bytes=GRANT - 153 * rows * columns * 4 // 10),
        cost_estimate=pl.CostEstimate(
            flops=4 * rows * columns * DH, bytes_accessed=24 * rows * columns, transcendentals=0
        ),
        name="states_own",
    )(queries, keys, values, prefix_state)


def columns_kernel(heads, levels, buckets, line_ref, weight_ref):
    half = heads // 2
    position = lax.axis_index("seq")
    own_second = lax.rem(position, 2) == 0
    rows = line_ref.shape[1]
    lines = []
    for i in range(levels):
        line = line_ref[i * heads : (i + 1) * heads]
        if i:
            line = line * lax.rem(lax.shift_right_logical(position, i - 1), 2).astype(F32)
        lines.append(jnp.where(own_second, jnp.concatenate([line[half:], line[:half]], axis=0), line))
    first = line_ref[heads * levels : heads * levels + half * buckets]
    second = line_ref[heads * levels + half * buckets :]
    lines.append(jnp.where(own_second, second, first))
    lines.append(jnp.where(own_second, first, second))
    spare = weight_ref.shape[1] - heads * (levels + buckets)
    if spare:
        lines.append(jnp.zeros((spare, rows), F32))
    weight_ref[...] = jnp.transpose(jnp.concatenate(lines, axis=0))


def weight_columns(level_weight, prefix_weight):
    heads, _, rows = level_weight.shape
    weights = heads * (level_weight.shape[1] + prefix_weight.shape[1])
    lines = jnp.concatenate(
        [
            jnp.transpose(level_weight, (1, 0, 2)).reshape(-1, rows),
            prefix_weight.reshape(-1, rows),
        ],
        axis=0,
    )
    shape = (rows, pl.cdiv(weights, DH) * DH)
    return pl.pallas_call(
        functools.partial(columns_kernel, heads, level_weight.shape[1], prefix_weight.shape[1]),
        out_shape=jax.ShapeDtypeStruct(shape, F32),
        in_specs=[IN_VMEM],
        out_specs=IN_VMEM,
        compiler_params=pltpu.CompilerParams(vmem_limit_bytes=GRANT // 4),
        cost_estimate=pl.CostEstimate(flops=0, bytes_accessed=8 * rows * DH, transcendentals=0),
        name="columns",
    )(lines)


def base_kernel(place, levels, buckets, offset, q_ref, k_ref, v_ref, weight_ref, prefix_ref, *refs):
    rows = q_ref.shape[0]
    heads = q_ref.shape[1] // DH
    per = heads // (2 * PARTS)
    copy = None
    if len(refs) > 1:
        prefix_hbm, out_ref, next_ref, sem = refs
        following = pl.ds(first_head(place + 1, per), next_ref.shape[0])
        copy = pltpu.make_async_copy(prefix_hbm.at[following], next_ref, sem)
        copy.start()
    else:
        (out_ref,) = refs
    row = lax.broadcasted_iota(jnp.int32, (rows, rows), 0)
    column = lax.broadcasted_iota(jnp.int32, (rows, rows), 1)
    nt = (((1,), (1,)), ((), ()))
    for j in range(per):
        head = place * per + j
        at = slice(head * DH, (head + 1) * DH)
        q, k, v = q_ref[:, at], k_ref[:, at], v_ref[:, at]
        k_high, k_low = split(k)
        q_wide = beside(q)
        scores = lax.dot_general(
            q_wide, jnp.concatenate([k_high, k_high], axis=1), nt, preferred_element_type=F32
        ) + lax.dot_general(
            q_wide, jnp.concatenate([k_low, k_low], axis=1), nt, preferred_element_type=F32
        )
        scores = jnp.where(column <= row, scores, 0.0) * weight_ref[:, head : head + 1]
        scores_high, scores_low = split(scores)
        v_wide = beside(v)
        total = jnp.dot(scores_high, v_wide, preferred_element_type=F32)
        total += jnp.dot(scores_low, v_wide, preferred_element_type=F32)
        for b in range(buckets):
            line = heads * levels + head * buckets + b
            total += through_state(
                q * weight_ref[:, line : line + 1], prefix_ref[offset + j, b * DH : (b + 1) * DH, :]
            )
        out_ref[:, j * DH : (j + 1) * DH] = fold_columns(total)
    if copy is not None:
        copy.wait()


def base_part(place, levels, buckets, loaded, prefix, prefix_state):
    rows, columns = loaded[0].shape
    per = columns // DH // (2 * PARTS)
    more = place < PARTS
    offset = max(place - PARTS, 0) * per
    ahead = PARTS * per if place == PARTS - 1 else per
    shapes = [(rows, per * DH)] + [(ahead, *prefix.shape[1:])] * more
    return pl.pallas_call(
        functools.partial(base_kernel, place, levels, buckets, offset),
        out_shape=[jax.ShapeDtypeStruct(s, F32) for s in shapes],
        in_specs=[IN_VMEM] * (len(loaded) + 1) + [IN_HBM] * more,
        out_specs=[IN_VMEM] * len(shapes),
        scratch_shapes=[pltpu.SemaphoreType.DMA] * more,
        compiler_params=pltpu.CompilerParams(vmem_limit_bytes=GRANT - 185 * rows * columns * 4 // 10),
        cost_estimate=pl.CostEstimate(
            flops=2 * per * DH * rows * rows * 24,
            bytes_accessed=20 * rows * per * DH,
            transcendentals=0,
        ),
    )(*loaded, prefix, *[prefix_state] * more)


def levels_kernel(places, terms, states, store, q_ref, weight_ref, *refs):
    state_refs, refs = refs[:states], refs[states:]
    base_refs, refs = refs[: len(places)], refs[len(places) :]
    per = base_refs[0].shape[1] // DH
    heads = q_ref.shape[1] // DH
    if store:
        out_hbm, buf, sems = refs[-3:]
    copies = []
    for c, place in enumerate(places):
        for j in range(per):
            at = slice(j * DH, (j + 1) * DH)
            head = place * per + j
            q = q_ref[:, head * DH : (head + 1) * DH]
            total = None
            for level, ref, entry in terms[c]:
                column = level * heads + head
                term = through_state(q * weight_ref[:, column : column + 1], state_refs[ref][entry + j])
                total = term if total is None else total + term
            done = base_refs[c][:, at]
            if total is not None:
                done += fold_columns(total)
            if store:
                buf[c, :, at] = done
            else:
                refs[c][:, at] = done
        if store:
            columns = head_columns(first_head(place, per), per)
            copy = pltpu.make_async_copy(buf.at[c], out_hbm.at[:, columns], sems.at[c])
            copy.start()
            copies.append(copy)
    for copy in copies:
        copy.wait()


def add_levels(queries, weights, bases, states, terms, places, store, out):
    rows, columns = queries.shape
    width = columns // (2 * PARTS)
    count = len(places)
    operands = [queries, weights, *states, *bases]
    in_specs = [IN_VMEM] * len(operands)
    aliases = {}
    if out is not None:
        aliases = {len(operands): 0}
        operands.append(out)
        in_specs.append(IN_HBM)
    shape = (rows, columns) if store else (rows, width)
    return pl.pallas_call(
        functools.partial(levels_kernel, places, terms, len(states), store),
        out_shape=[jax.ShapeDtypeStruct(shape, F32)] * (1 if store else count),
        in_specs=in_specs,
        out_specs=[IN_HBM if store else IN_VMEM] * (1 if store else count),
        scratch_shapes=[pltpu.VMEM((count, rows, width), F32), pltpu.SemaphoreType.DMA((count,))]
        if store
        else [],
        input_output_aliases=aliases,
        compiler_params=pltpu.CompilerParams(vmem_limit_bytes=GRANT // 4),
        cost_estimate=pl.CostEstimate(
            flops=4 * width * rows * rows * sum(len(t) for t in terms),
            bytes_accessed=12 * rows * width * count,
            transcendentals=0,
        ),
    )(*operands)


def swapped(array, bit, needs=None):
    size, cores = lax.axis_size("seq"), lax.axis_size("head")
    pairs = []
    for i in range(size):
        for core in range(cores):
            if needs is None or needs(i) or cores % 2:
                to = (i ^ 1 << bit) * cores + core
            else:
                to = i * cores + (core ^ 1)
            pairs.append((i * cores + core, to))
    return lax.ppermute(array, ("seq", "head"), pairs)


def attend(queries, keys, values, level_weight, prefix_weight, prefix_state):
    levels = lax.axis_size("seq").bit_length() - 1
    per = queries.shape[1] // DH // (2 * PARTS)
    places = range(PARTS)

    given = [given_states(keys, values)]
    *loaded, prefix, own, part0, part1, rest = own_block_states(queries, keys, values, prefix_state)
    weights = weight_columns(level_weight, prefix_weight)
    given.append(rest)
    received = [swapped(given[c], 0) for c in places]
    parts = (part0, part1)
    loaded.append(weights)
    query_places = loaded[0]
    base = []
    for place in range(2 * PARTS):
        done, *following = base_part(place, level_weight.shape[1], prefix_weight.shape[1], loaded, prefix, prefix_state)
        base.append(done)
        if following:
            (prefix,) = following

    own_states = [list(received)]
    running = [parts[c] + received[c] for c in places]
    for bit in range(1, levels):
        arrived = [swapped(running[c], bit) for c in places]
        own_states.append(arrived)
        running = [a + b for a, b in zip(running, arrived)]
    other_states = [[swapped(own, 0)]]
    for bit in range(1, levels - 1):
        both = jnp.concatenate(own_states[bit], axis=0)
        other_states.append([swapped(both, 0)])
    top = levels - 1
    needs = lambda i: i >> top & 1
    last = [swapped(own_states[top][c], 0, needs if c in (0, 1) else None) for c in places]

    flat = [x for level in own_states for x in level]
    terms = [[(1 + i, i * PARTS + c, 0) for i in range(levels)] for c in places]
    (out,) = add_levels(query_places, weights, base[:PARTS], flat, terms, tuple(places), True, None)
    flat = [x[0] for x in other_states] + last[:-1]
    terms = [[(1 + i, i, c * per) for i in range(levels - 1)] for c in places]
    for c in places[:-1]:
        terms[c].append((levels, levels - 1 + c, 0))
    other = tuple(PARTS + c for c in places)
    middle = add_levels(query_places, weights, base[PARTS:], flat, terms, other, False, None)
    terms = [[] for _ in places[:-1]] + [[(levels, 0, 0)]]
    (out,) = add_levels(query_places, weights, middle, last[-1:], terms, other, True, out)
    return out


def solution(mesh):
    return jax.shard_map(
        attend,
        mesh=mesh,
        in_specs=(
            P(("groups", "seq"), "head"),
            P(("groups", "seq"), "head"),
            P(("groups", "seq"), "head"),
            P("head", None, ("groups", "seq")),
            P("head", None, ("groups", "seq")),
            P("head", "groups", None),
        ),
        out_specs=P(("groups", "seq"), "head"),
        check_vma=False,
    )
```

```python
import functools

import jax
import jax.numpy as jnp
from jax import lax
from jax.experimental import pallas as pl
from jax.experimental.pallas import tpu as pltpu
from jax.sharding import PartitionSpec as P

DH = 128
BF16 = jnp.bfloat16
F32 = jnp.float32
PARTS = 2
GRANT = 67043328
IN_VMEM = pl.BlockSpec(memory_space=pltpu.VMEM)
IN_HBM = pl.BlockSpec(memory_space=pltpu.HBM)


def split(x):
    high = x.astype(BF16)
    low = (x - high.astype(F32)).astype(BF16)
    return high, low


def beside(x):
    return jnp.concatenate(split(x), axis=1)


def fold_columns(x):
    half = x.shape[1] // 2
    return x[:, :half] + x[:, half:]


def outer_state(k, v):
    full = lax.dot_general(
        beside(k), beside(v), (((0,), (0,)), ((), ())), preferred_element_type=F32
    )
    full = fold_columns(full)
    return full[:DH] + full[DH:]


def through_state(scaled, state):
    wide = beside(state)
    return jnp.dot(
        beside(scaled), jnp.concatenate([wide, wide], axis=0), preferred_element_type=F32
    )


def first_head(place, per):
    own = 1 - lax.rem(lax.axis_index("seq"), 2)
    half = own if place < PARTS else 1 - own
    return (half * PARTS + place % PARTS) * per


def head_columns(head, count=1):
    return pl.ds(pl.multiple_of(head * DH, DH), count * DH)


def given_kernel(place, k_hbm, v_hbm, out_ref, k_buf, v_buf, sems):
    per = out_ref.shape[0]
    columns = head_columns(first_head(place, per), per)
    copies = (
        pltpu.make_async_copy(k_hbm.at[:, columns], k_buf, sems.at[0]),
        pltpu.make_async_copy(v_hbm.at[:, columns], v_buf, sems.at[1]),
    )
    for copy in copies:
        copy.start()
    for copy in copies:
        copy.wait()
    for j in range(per):
        at = slice(j * DH, (j + 1) * DH)
        out_ref[j] = outer_state(k_buf[:, at], v_buf[:, at])


def given_states(keys, values):
    rows, columns = keys.shape
    width = columns // (2 * PARTS)
    return pl.pallas_call(
        functools.partial(given_kernel, PARTS),
        out_shape=jax.ShapeDtypeStruct((width // DH, DH, DH), F32),
        in_specs=[IN_HBM] * 2,
        out_specs=IN_VMEM,
        scratch_shapes=[
            pltpu.VMEM((rows, width), F32),
            pltpu.VMEM((rows, width), F32),
            pltpu.SemaphoreType.DMA((2,)),
        ],
        compiler_params=pltpu.CompilerParams(vmem_limit_bytes=GRANT - 105 * rows * columns * 4 // 10),
        cost_estimate=pl.CostEstimate(
            flops=2 * rows * columns * DH, bytes_accessed=2 * rows * columns, transcendentals=0
        ),
        name="states_given",
    )(keys, values)


def own_kernel(
    q_hbm, k_hbm, v_hbm, prefix_hbm,
    q_out, k_out, v_out, prefix_out, whole_ref, *refs,
):
    (*part_refs, given_ref), sems = refs[:-1], refs[-1]
    per = given_ref.shape[0]
    half = PARTS * per
    copies = []
    for i, (source, to) in enumerate(((k_hbm, k_out), (v_hbm, v_out), (q_hbm, q_out))):
        for h in range(2):
            copy = pltpu.make_async_copy(
                source.at[:, head_columns(first_head(h * PARTS, per), half)],
                to.at[:, h * half * DH : (h + 1) * half * DH],
                sems.at[i, h],
            )
            copy.start()
            copies.append(copy)
    copies.append(
        pltpu.make_async_copy(prefix_hbm.at[pl.ds(first_head(0, per), per)], prefix_out, sems.at[3, 0])
    )
    copies[-1].start()
    copies[1].wait()
    copies[3].wait()
    for j in range(per):
        head = half + (PARTS - 1) * per + j
        at = slice(head * DH, (head + 1) * DH)
        given_ref[j] = outer_state(k_out[:, at], v_out[:, at])
    copies[0].wait()
    copies[2].wait()
    for c, part_ref in enumerate(part_refs):
        for j in range(per):
            at = slice((c * per + j) * DH, (c * per + j + 1) * DH)
            state = outer_state(k_out[:, at], v_out[:, at])
            part_ref[j] = state
            whole_ref[c * per + j] = state
    for i in (4, 5, 6):
        copies[i].wait()


def own_block_states(queries, keys, values, prefix_state):
    rows, columns = keys.shape
    heads = columns // DH
    per = heads // (2 * PARTS)
    shapes = [queries.shape, keys.shape, values.shape, (per, *prefix_state.shape[1:])]
    shapes += [(PARTS * per, DH, DH)] + [(per, DH, DH)] * (PARTS + 1)
    return pl.pallas_call(
        own_kernel,
        out_shape=[jax.ShapeDtypeStruct(s, F32) for s in shapes],
        in_specs=[IN_HBM] * 4,
        out_specs=[IN_VMEM] * len(shapes),
        scratch_shapes=[pltpu.SemaphoreType.DMA((4, 2))],
        compiler_params=pltpu.CompilerParams(vmem_limit_bytes=GRANT - 153 * rows * columns * 4 // 10),
        cost_estimate=pl.CostEstimate(
            flops=4 * rows * columns * DH, bytes_accessed=24 * rows * columns, transcendentals=0
        ),
        name="states_own",
    )(queries, keys, values, prefix_state)


def columns_kernel(heads, levels, buckets, line_ref, weight_ref):
    half = heads // 2
    position = lax.axis_index("seq")
    own_second = lax.rem(position, 2) == 0
    rows = line_ref.shape[1]
    lines = []
    for i in range(levels):
        line = line_ref[i * heads : (i + 1) * heads]
        if i:
            line = line * lax.rem(lax.shift_right_logical(position, i - 1), 2).astype(F32)
        lines.append(jnp.where(own_second, jnp.concatenate([line[half:], line[:half]], axis=0), line))
    first = line_ref[heads * levels : heads * levels + half * buckets]
    second = line_ref[heads * levels + half * buckets :]
    lines.append(jnp.where(own_second, second, first))
    lines.append(jnp.where(own_second, first, second))
    spare = weight_ref.shape[1] - heads * (levels + buckets)
    if spare:
        lines.append(jnp.zeros((spare, rows), F32))
    weight_ref[...] = jnp.transpose(jnp.concatenate(lines, axis=0))


def weight_columns(level_weight, prefix_weight):
    heads, _, rows = level_weight.shape
    weights = heads * (level_weight.shape[1] + prefix_weight.shape[1])
    lines = jnp.concatenate(
        [
            jnp.transpose(level_weight, (1, 0, 2)).reshape(-1, rows),
            prefix_weight.reshape(-1, rows),
        ],
        axis=0,
    )
    shape = (rows, pl.cdiv(weights, DH) * DH)
    return pl.pallas_call(
        functools.partial(columns_kernel, heads, level_weight.shape[1], prefix_weight.shape[1]),
        out_shape=jax.ShapeDtypeStruct(shape, F32),
        in_specs=[IN_VMEM],
        out_specs=IN_VMEM,
        compiler_params=pltpu.CompilerParams(vmem_limit_bytes=GRANT // 4),
        cost_estimate=pl.CostEstimate(flops=0, bytes_accessed=8 * rows * DH, transcendentals=0),
        name="columns",
    )(lines)


def base_kernel(place, levels, buckets, offset, q_ref, k_ref, v_ref, weight_ref, prefix_ref, *refs):
    rows = q_ref.shape[0]
    heads = q_ref.shape[1] // DH
    per = heads // (2 * PARTS)
    copy = None
    if len(refs) > 1:
        prefix_hbm, out_ref, next_ref, sem = refs
        following = pl.ds(first_head(place + 1, per), next_ref.shape[0])
        copy = pltpu.make_async_copy(prefix_hbm.at[following], next_ref, sem)
        copy.start()
    else:
        (out_ref,) = refs
    row = lax.broadcasted_iota(jnp.int32, (rows, rows), 0)
    column = lax.broadcasted_iota(jnp.int32, (rows, rows), 1)
    nt = (((1,), (1,)), ((), ()))
    for j in range(per):
        head = place * per + j
        at = slice(head * DH, (head + 1) * DH)
        q, k, v = q_ref[:, at], k_ref[:, at], v_ref[:, at]
        k_high, k_low = split(k)
        q_wide = beside(q)
        scores = lax.dot_general(
            q_wide, jnp.concatenate([k_high, k_high], axis=1), nt, preferred_element_type=F32
        ) + lax.dot_general(
            q_wide, jnp.concatenate([k_low, k_low], axis=1), nt, preferred_element_type=F32
        )
        scores = jnp.where(column <= row, scores, 0.0) * weight_ref[:, head : head + 1]
        scores_high, scores_low = split(scores)
        v_wide = beside(v)
        total = jnp.dot(scores_high, v_wide, preferred_element_type=F32)
        total += jnp.dot(scores_low, v_wide, preferred_element_type=F32)
        for b in range(buckets):
            line = heads * levels + head * buckets + b
            total += through_state(
                q * weight_ref[:, line : line + 1], prefix_ref[offset + j, b * DH : (b + 1) * DH, :]
            )
        out_ref[:, j * DH : (j + 1) * DH] = fold_columns(total)
    if copy is not None:
        copy.wait()


def base_part(place, levels, buckets, loaded, prefix, prefix_state):
    rows, columns = loaded[0].shape
    per = columns // DH // (2 * PARTS)
    more = place < PARTS
    offset = max(place - PARTS, 0) * per
    ahead = PARTS * per if place == PARTS - 1 else per
    shapes = [(rows, per * DH)] + [(ahead, *prefix.shape[1:])] * more
    return pl.pallas_call(
        functools.partial(base_kernel, place, levels, buckets, offset),
        out_shape=[jax.ShapeDtypeStruct(s, F32) for s in shapes],
        in_specs=[IN_VMEM] * (len(loaded) + 1) + [IN_HBM] * more,
        out_specs=[IN_VMEM] * len(shapes),
        scratch_shapes=[pltpu.SemaphoreType.DMA] * more,
        compiler_params=pltpu.CompilerParams(vmem_limit_bytes=GRANT - 185 * rows * columns * 4 // 10),
        cost_estimate=pl.CostEstimate(
            flops=2 * per * DH * rows * rows * 24,
            bytes_accessed=20 * rows * per * DH,
            transcendentals=0,
        ),
    )(*loaded, prefix, *[prefix_state] * more)


def levels_kernel(places, terms, states, store, q_ref, weight_ref, *refs):
    state_refs, refs = refs[:states], refs[states:]
    base_refs, refs = refs[: len(places)], refs[len(places) :]
    per = base_refs[0].shape[1] // DH
    heads = q_ref.shape[1] // DH
    if store:
        out_hbm, buf, sems = refs[-3:]
    copies = []
    for c, place in enumerate(places):
        for j in range(per):
            at = slice(j * DH, (j + 1) * DH)
            head = place * per + j
            q = q_ref[:, head * DH : (head + 1) * DH]
            total = None
            for level, ref, entry in terms[c]:
                column = level * heads + head
                term = through_state(q * weight_ref[:, column : column + 1], state_refs[ref][entry + j])
                total = term if total is None else total + term
            done = base_refs[c][:, at]
            if total is not None:
                done += fold_columns(total)
            if store:
                buf[c, :, at] = done
                columns = head_columns(first_head(place, per) + j)
                copy = pltpu.make_async_copy(buf.at[c, :, at], out_hbm.at[:, columns], sems.at[c, j])
                copy.start()
                copies.append(copy)
            else:
                refs[c][:, at] = done
    for copy in copies:
        copy.wait()


def add_levels(queries, weights, bases, states, terms, places, store, out):
    rows, columns = queries.shape
    width = columns // (2 * PARTS)
    count = len(places)
    operands = [queries, weights, *states, *bases]
    in_specs = [IN_VMEM] * len(operands)
    aliases = {}
    if out is not None:
        aliases = {len(operands): 0}
        operands.append(out)
        in_specs.append(IN_HBM)
    shape = (rows, columns) if store else (rows, width)
    return pl.pallas_call(
        functools.partial(levels_kernel, places, terms, len(states), store),
        out_shape=[jax.ShapeDtypeStruct(shape, F32)] * (1 if store else count),
        in_specs=in_specs,
        out_specs=[IN_HBM if store else IN_VMEM] * (1 if store else count),
        scratch_shapes=[pltpu.VMEM((count, rows, width), F32), pltpu.SemaphoreType.DMA((count, width // DH))]
        if store
        else [],
        input_output_aliases=aliases,
        compiler_params=pltpu.CompilerParams(vmem_limit_bytes=GRANT // 4),
        cost_estimate=pl.CostEstimate(
            flops=4 * width * rows * rows * sum(len(t) for t in terms),
            bytes_accessed=12 * rows * width * count,
            transcendentals=0,
        ),
    )(*operands)


def swapped(array, bit, needs=None):
    size, cores = lax.axis_size("seq"), lax.axis_size("head")
    pairs = []
    for i in range(size):
        for core in range(cores):
            if needs is None or needs(i) or cores % 2:
                to = (i ^ 1 << bit) * cores + core
            else:
                to = i * cores + (core ^ 1)
            pairs.append((i * cores + core, to))
    return lax.ppermute(array, ("seq", "head"), pairs)


def attend(queries, keys, values, level_weight, prefix_weight, prefix_state):
    levels = lax.axis_size("seq").bit_length() - 1
    per = queries.shape[1] // DH // (2 * PARTS)
    places = range(PARTS)

    given = [given_states(keys, values)]
    *loaded, prefix, own, part0, part1, rest = own_block_states(queries, keys, values, prefix_state)
    weights = weight_columns(level_weight, prefix_weight)
    given.append(rest)
    received = [swapped(given[c], 0) for c in places]
    parts = (part0, part1)
    loaded.append(weights)
    query_places = loaded[0]
    base = []
    for place in range(2 * PARTS):
        done, *following = base_part(place, level_weight.shape[1], prefix_weight.shape[1], loaded, prefix, prefix_state)
        base.append(done)
        if following:
            (prefix,) = following

    own_states = [list(received)]
    running = [parts[c] + received[c] for c in places]
    for bit in range(1, levels):
        arrived = [swapped(running[c], bit) for c in places]
        own_states.append(arrived)
        running = [a + b for a, b in zip(running, arrived)]
    other_states = [[swapped(own, 0)]]
    for bit in range(1, levels - 1):
        both = jnp.concatenate(own_states[bit], axis=0)
        other_states.append([swapped(both, 0)])
    top = levels - 1
    needs = lambda i: i >> top & 1
    last = [swapped(own_states[top][c], 0, needs if c in (0, 1) else None) for c in places]

    flat = [x for level in own_states for x in level]
    terms = [[(1 + i, i * PARTS + c, 0) for i in range(levels)] for c in places]
    (out,) = add_levels(query_places, weights, base[:PARTS], flat, terms, tuple(places), True, None)
    flat = [x[0] for x in other_states] + last[:-1]
    terms = [[(1 + i, i, c * per) for i in range(levels - 1)] for c in places]
    for c in places[:-1]:
        terms[c].append((levels, levels - 1 + c, 0))
    other = tuple(PARTS + c for c in places)
    middle = add_levels(query_places, weights, base[PARTS:], flat, terms, other, False, None)
    terms = [[] for _ in places[:-1]] + [[(levels, 0, 0)]]
    (out,) = add_levels(query_places, weights, middle, last[-1:], terms, other, True, out)
    return out


def solution(mesh):
    return jax.shard_map(
        attend,
        mesh=mesh,
        in_specs=(
            P(("groups", "seq"), "head"),
            P(("groups", "seq"), "head"),
            P(("groups", "seq"), "head"),
            P("head", None, ("groups", "seq")),
            P("head", None, ("groups", "seq")),
            P("head", "groups", None),
        ),
        out_specs=P(("groups", "seq"), "head"),
        check_vma=False,
    )
```

```python
import functools

import jax
import jax.numpy as jnp
from jax import lax
from jax.experimental import pallas as pl
from jax.experimental.pallas import tpu as pltpu
from jax.sharding import PartitionSpec as P

DH = 128
BF16 = jnp.bfloat16
F32 = jnp.float32
PARTS = 2
GRANT = 67043328
IN_VMEM = pl.BlockSpec(memory_space=pltpu.VMEM)
IN_HBM = pl.BlockSpec(memory_space=pltpu.HBM)


def split(x):
    high = x.astype(BF16)
    low = (x - high.astype(F32)).astype(BF16)
    return high, low


def beside(x):
    return jnp.concatenate(split(x), axis=1)


def fold_columns(x):
    half = x.shape[1] // 2
    return x[:, :half] + x[:, half:]


def outer_state(k, v):
    full = lax.dot_general(
        beside(k), beside(v), (((0,), (0,)), ((), ())), preferred_element_type=F32
    )
    full = fold_columns(full)
    return full[:DH] + full[DH:]


def through_state(scaled, state):
    wide = beside(state)
    return jnp.dot(
        beside(scaled), jnp.concatenate([wide, wide], axis=0), preferred_element_type=F32
    )


def first_head(place, per):
    own = 1 - lax.rem(lax.axis_index("seq"), 2)
    half = own if place < PARTS else 1 - own
    return (half * PARTS + place % PARTS) * per


def head_columns(head, count=1):
    return pl.ds(pl.multiple_of(head * DH, DH), count * DH)


def given_kernel(place, k_hbm, v_hbm, out_ref, k_buf, v_buf, sems):
    per = out_ref.shape[0]
    columns = head_columns(first_head(place, per), per)
    copies = (
        pltpu.make_async_copy(k_hbm.at[:, columns], k_buf, sems.at[0]),
        pltpu.make_async_copy(v_hbm.at[:, columns], v_buf, sems.at[1]),
    )
    for copy in copies:
        copy.start()
    for copy in copies:
        copy.wait()
    for j in range(per):
        at = slice(j * DH, (j + 1) * DH)
        out_ref[j] = outer_state(k_buf[:, at], v_buf[:, at])


def given_states(keys, values):
    rows, columns = keys.shape
    width = columns // (2 * PARTS)
    return pl.pallas_call(
        functools.partial(given_kernel, PARTS),
        out_shape=jax.ShapeDtypeStruct((width // DH, DH, DH), F32),
        in_specs=[IN_HBM] * 2,
        out_specs=IN_VMEM,
        scratch_shapes=[
            pltpu.VMEM((rows, width), F32),
            pltpu.VMEM((rows, width), F32),
            pltpu.SemaphoreType.DMA((2,)),
        ],
        compiler_params=pltpu.CompilerParams(vmem_limit_bytes=GRANT - 105 * rows * columns * 4 // 10),
        cost_estimate=pl.CostEstimate(
            flops=2 * rows * columns * DH, bytes_accessed=2 * rows * columns, transcendentals=0
        ),
        name="states_given",
    )(keys, values)


def own_kernel(
    q_hbm, k_hbm, v_hbm, prefix_hbm,
    q_out, k_out, v_out, prefix_out, whole_ref, *refs,
):
    (*part_refs, given_ref), sems = refs[:-1], refs[-1]
    per = given_ref.shape[0]
    half = PARTS * per
    copies = []
    for i, (source, to) in enumerate(((k_hbm, k_out), (v_hbm, v_out), (q_hbm, q_out))):
        for h in range(2):
            copy = pltpu.make_async_copy(
                source.at[:, head_columns(first_head(h * PARTS, per), half)],
                to.at[:, h * half * DH : (h + 1) * half * DH],
                sems.at[i, h],
            )
            copy.start()
            copies.append(copy)
    copies.append(
        pltpu.make_async_copy(prefix_hbm.at[pl.ds(first_head(0, per), per)], prefix_out, sems.at[3, 0])
    )
    copies[-1].start()
    copies[1].wait()
    copies[3].wait()
    for j in range(per):
        head = half + (PARTS - 1) * per + j
        at = slice(head * DH, (head + 1) * DH)
        given_ref[j] = outer_state(k_out[:, at], v_out[:, at])
    copies[0].wait()
    copies[2].wait()
    for c, part_ref in enumerate(part_refs):
        for j in range(per):
            at = slice((c * per + j) * DH, (c * per + j + 1) * DH)
            state = outer_state(k_out[:, at], v_out[:, at])
            part_ref[j] = state
            whole_ref[c * per + j] = state
    for i in (4, 5, 6):
        copies[i].wait()


def own_block_states(queries, keys, values, prefix_state):
    rows, columns = keys.shape
    heads = columns // DH
    per = heads // (2 * PARTS)
    shapes = [queries.shape, keys.shape, values.shape, (per, *prefix_state.shape[1:])]
    shapes += [(PARTS * per, DH, DH)] + [(per, DH, DH)] * (PARTS + 1)
    return pl.pallas_call(
        own_kernel,
        out_shape=[jax.ShapeDtypeStruct(s, F32) for s in shapes],
        in_specs=[IN_HBM] * 4,
        out_specs=[IN_VMEM] * len(shapes),
        scratch_shapes=[pltpu.SemaphoreType.DMA((4, 2))],
        compiler_params=pltpu.CompilerParams(vmem_limit_bytes=GRANT - 153 * rows * columns * 4 // 10),
        cost_estimate=pl.CostEstimate(
            flops=4 * rows * columns * DH, bytes_accessed=24 * rows * columns, transcendentals=0
        ),
        name="states_own",
    )(queries, keys, values, prefix_state)


def columns_kernel(heads, levels, buckets, line_ref, weight_ref):
    half = heads // 2
    position = lax.axis_index("seq")
    own_second = lax.rem(position, 2) == 0
    rows = line_ref.shape[1]
    lines = []
    for i in range(levels):
        line = line_ref[i * heads : (i + 1) * heads]
        if i:
            line = line * lax.rem(lax.shift_right_logical(position, i - 1), 2).astype(F32)
        lines.append(jnp.where(own_second, jnp.concatenate([line[half:], line[:half]], axis=0), line))
    first = line_ref[heads * levels : heads * levels + half * buckets]
    second = line_ref[heads * levels + half * buckets :]
    lines.append(jnp.where(own_second, second, first))
    lines.append(jnp.where(own_second, first, second))
    spare = weight_ref.shape[1] - heads * (levels + buckets)
    if spare:
        lines.append(jnp.zeros((spare, rows), F32))
    weight_ref[...] = jnp.transpose(jnp.concatenate(lines, axis=0))


def weight_columns(level_weight, prefix_weight):
    heads, _, rows = level_weight.shape
    weights = heads * (level_weight.shape[1] + prefix_weight.shape[1])
    lines = jnp.concatenate(
        [
            jnp.transpose(level_weight, (1, 0, 2)).reshape(-1, rows),
            prefix_weight.reshape(-1, rows),
        ],
        axis=0,
    )
    shape = (rows, pl.cdiv(weights, DH) * DH)
    return pl.pallas_call(
        functools.partial(columns_kernel, heads, level_weight.shape[1], prefix_weight.shape[1]),
        out_shape=jax.ShapeDtypeStruct(shape, F32),
        in_specs=[IN_VMEM],
        out_specs=IN_VMEM,
        compiler_params=pltpu.CompilerParams(vmem_limit_bytes=GRANT // 4),
        cost_estimate=pl.CostEstimate(flops=0, bytes_accessed=8 * rows * DH, transcendentals=0),
        name="columns",
    )(lines)


def base_kernel(place, levels, buckets, offset, q_ref, k_ref, v_ref, weight_ref, prefix_ref, *refs):
    rows = q_ref.shape[0]
    heads = q_ref.shape[1] // DH
    per = heads // (2 * PARTS)
    copy = None
    if len(refs) > 1:
        prefix_hbm, out_ref, next_ref, sem = refs
        following = pl.ds(first_head(place + 1, per), next_ref.shape[0])
        copy = pltpu.make_async_copy(prefix_hbm.at[following], next_ref, sem)
        copy.start()
    else:
        (out_ref,) = refs
    row = lax.broadcasted_iota(jnp.int32, (rows, rows), 0)
    column = lax.broadcasted_iota(jnp.int32, (rows, rows), 1)
    nt = (((1,), (1,)), ((), ()))
    for j in range(per):
        head = place * per + j
        at = slice(head * DH, (head + 1) * DH)
        q, k, v = q_ref[:, at], k_ref[:, at], v_ref[:, at]
        k_high, k_low = split(k)
        q_wide = beside(q)
        scores = lax.dot_general(
            q_wide, jnp.concatenate([k_high, k_high], axis=1), nt, preferred_element_type=F32
        ) + lax.dot_general(
            q_wide, jnp.concatenate([k_low, k_low], axis=1), nt, preferred_element_type=F32
        )
        scores = jnp.where(column <= row, scores, 0.0) * weight_ref[:, head : head + 1]
        scores_high, scores_low = split(scores)
        v_wide = beside(v)
        total = jnp.dot(scores_high, v_wide, preferred_element_type=F32)
        total += jnp.dot(scores_low, v_wide, preferred_element_type=F32)
        for b in range(buckets):
            line = heads * levels + head * buckets + b
            total += through_state(
                q * weight_ref[:, line : line + 1], prefix_ref[offset + j, b * DH : (b + 1) * DH, :]
            )
        out_ref[:, j * DH : (j + 1) * DH] = fold_columns(total)
    if copy is not None:
        copy.wait()


def base_part(place, levels, buckets, loaded, prefix, prefix_state):
    rows, columns = loaded[0].shape
    per = columns // DH // (2 * PARTS)
    more = place < PARTS
    offset = max(place - PARTS, 0) * per
    ahead = PARTS * per if place == PARTS - 1 else per
    shapes = [(rows, per * DH)] + [(ahead, *prefix.shape[1:])] * more
    return pl.pallas_call(
        functools.partial(base_kernel, place, levels, buckets, offset),
        out_shape=[jax.ShapeDtypeStruct(s, F32) for s in shapes],
        in_specs=[IN_VMEM] * (len(loaded) + 1) + [IN_HBM] * more,
        out_specs=[IN_VMEM] * len(shapes),
        scratch_shapes=[pltpu.SemaphoreType.DMA] * more,
        compiler_params=pltpu.CompilerParams(vmem_limit_bytes=GRANT - 185 * rows * columns * 4 // 10),
        cost_estimate=pl.CostEstimate(
            flops=2 * per * DH * rows * rows * 24,
            bytes_accessed=20 * rows * per * DH,
            transcendentals=0,
        ),
    )(*loaded, prefix, *[prefix_state] * more)


def levels_kernel(places, terms, states, store, q_ref, weight_ref, *refs):
    state_refs, refs = refs[:states], refs[states:]
    base_refs, refs = refs[: len(places)], refs[len(places) :]
    per = base_refs[0].shape[1] // DH
    heads = q_ref.shape[1] // DH
    if store:
        out_hbm, buf, sems = refs[-3:]
    copies = []
    for c, place in enumerate(places):
        for j in range(per):
            at = slice(j * DH, (j + 1) * DH)
            head = place * per + j
            q = q_ref[:, head * DH : (head + 1) * DH]
            total = None
            for level, ref, entry in terms[c]:
                column = level * heads + head
                term = through_state(q * weight_ref[:, column : column + 1], state_refs[ref][entry + j])
                total = term if total is None else total + term
            done = base_refs[c][:, at]
            if total is not None:
                done += fold_columns(total)
            if store:
                buf[c, :, at] = done
            else:
                refs[c][:, at] = done
        if store:
            columns = head_columns(first_head(place, per), per)
            copy = pltpu.make_async_copy(buf.at[c], out_hbm.at[:, columns], sems.at[c])
            copy.start()
            copies.append(copy)
    for copy in copies:
        copy.wait()


def add_levels(queries, weights, bases, states, terms, places, store, out):
    rows, columns = queries.shape
    width = columns // (2 * PARTS)
    count = len(places)
    operands = [queries, weights, *states, *bases]
    in_specs = [IN_VMEM] * len(operands)
    aliases = {}
    if out is not None:
        aliases = {len(operands): 0}
        operands.append(out)
        in_specs.append(IN_HBM)
    shape = (rows, columns) if store else (rows, width)
    return pl.pallas_call(
        functools.partial(levels_kernel, places, terms, len(states), store),
        out_shape=[jax.ShapeDtypeStruct(shape, F32)] * (1 if store else count),
        in_specs=in_specs,
        out_specs=[IN_HBM if store else IN_VMEM] * (1 if store else count),
        scratch_shapes=[pltpu.VMEM((count, rows, width), F32), pltpu.SemaphoreType.DMA((count,))]
        if store
        else [],
        input_output_aliases=aliases,
        compiler_params=pltpu.CompilerParams(vmem_limit_bytes=GRANT // 4),
        cost_estimate=pl.CostEstimate(
            flops=4 * width * rows * rows * sum(len(t) for t in terms),
            bytes_accessed=12 * rows * width * count,
            transcendentals=0,
        ),
    )(*operands)


def swapped(array, bit, needs=None, cross=False):
    size, cores = lax.axis_size("seq"), lax.axis_size("head")
    pairs = []
    for i in range(size):
        for core in range(cores):
            if needs is None or needs(i) or cores % 2:
                to = (i ^ (3 << bit - 1 if cross and core % 2 == 0 else 1 << bit)) * cores + core
            else:
                to = i * cores + (core ^ 1)
            pairs.append((i * cores + core, to))
    return lax.ppermute(array, ("seq", "head"), pairs)


def attend(queries, keys, values, level_weight, prefix_weight, prefix_state):
    levels = lax.axis_size("seq").bit_length() - 1
    per = queries.shape[1] // DH // (2 * PARTS)
    places = range(PARTS)

    given = [given_states(keys, values)]
    *loaded, prefix, own, part0, part1, rest = own_block_states(queries, keys, values, prefix_state)
    weights = weight_columns(level_weight, prefix_weight)
    given.append(rest)
    received = [swapped(given[c], 0) for c in places]
    parts = (part0, part1)
    loaded.append(weights)
    query_places = loaded[0]
    base = []
    for place in range(2 * PARTS):
        done, *following = base_part(place, level_weight.shape[1], prefix_weight.shape[1], loaded, prefix, prefix_state)
        base.append(done)
        if following:
            (prefix,) = following

    own_states = [list(received)]
    running = [parts[c] + received[c] for c in places]
    for bit in range(1, levels):
        arrived = [swapped(running[c], bit, cross=bit > 1 and c == PARTS - 1) for c in places]
        own_states.append(arrived)
        running = [a + b for a, b in zip(running, arrived)]
    other_states = [[swapped(own, 0)]]
    for bit in range(1, levels - 1):
        both = jnp.concatenate(own_states[bit], axis=0)
        other_states.append([swapped(both, 0, lambda i, bit=bit: i >> bit & 1)])
    top = levels - 1
    needs = lambda i: i >> top & 1
    last = [swapped(own_states[top][c], 0, needs if c in (0, 1) else None) for c in places]

    flat = [x for level in own_states for x in level]
    terms = [[(1 + i, i * PARTS + c, 0) for i in range(levels)] for c in places]
    (out,) = add_levels(query_places, weights, base[:PARTS], flat, terms, tuple(places), True, None)
    flat = [x[0] for x in other_states] + last[:-1]
    terms = [[(1 + i, i, c * per) for i in range(levels - 1)] for c in places]
    for c in places[:-1]:
        terms[c].append((levels, levels - 1 + c, 0))
    other = tuple(PARTS + c for c in places)
    middle = add_levels(query_places, weights, base[PARTS:], flat, terms, other, False, None)
    terms = [[] for _ in places[:-1]] + [[(levels, 0, 0)]]
    (out,) = add_levels(query_places, weights, middle, last[-1:], terms, other, True, out)
    return out


def solution(mesh):
    return jax.shard_map(
        attend,
        mesh=mesh,
        in_specs=(
            P(("groups", "seq"), "head"),
            P(("groups", "seq"), "head"),
            P(("groups", "seq"), "head"),
            P("head", None, ("groups", "seq")),
            P("head", None, ("groups", "seq")),
            P("head", "groups", None),
        ),
        out_specs=P(("groups", "seq"), "head"),
        check_vma=False,
    )
```
